32 devices in a mesh: wide: 16 (over z, x, core), narrow: 2 (over y).
Axes of the slice: x: 2, y: 2, z: 4, core: 2. Of those that a mesh axis runs over, the one named last changes fastest.
Arguments:
- projections: float32 [8, 1152, 1152], P(None, 'wide', 'narrow'), may hold values from -0.1875 to 0.1875
- qkv_weights: float32 [2, 1152, 3456], P(None, 'wide', 'narrow'), may hold values from -0.1875 to 0.1875
- mlp_weights: float32 [2, 1152, 4608], P(None, 'wide', 'narrow'), may hold values from -0.1875 to 0.1875
- ada_weights: float32 [1152, 6912], P('wide', 'narrow'), may hold values from -0.1875 to 0.1875
- entry_weights: float32 [4352, 1152], P('wide', 'narrow'), may hold values from -0.09375 to 0.09375
- patch_weights: float32 [2, 1152, 16], P(None, 'wide', 'narrow'), may hold values from -1.5 to 1.5
- shift_tables: float32 [8, 1152], P('narrow', 'wide'), may hold values from -0.5 to 0.5
- first_projections: float32 [8, 1152, 1152], P(None, 'wide', 'narrow'), may hold values from -1.9073486e-06 to 1.9073486e-06
- first_qkv_weights: float32 [2, 1152, 3456], P(None, 'wide', 'narrow'), may hold values from -1.9073486e-06 to 1.9073486e-06
- first_mlp_weights: float32 [2, 1152, 4608], P(None, 'wide', 'narrow'), may hold values from -1.9073486e-06 to 1.9073486e-06
- first_ada_weights: float32 [1152, 6912], P('wide', 'narrow'), may hold values from -1.9073486e-06 to 1.9073486e-06
- first_entry_weights: float32 [4352, 1152], P('wide', 'narrow'), may hold values from -1.9073486e-06 to 1.9073486e-06
- first_patch_weights: float32 [2, 1152, 16], P(None, 'wide', 'narrow'), may hold values from -1.9073486e-06 to 1.9073486e-06
- first_shift_tables: float32 [8, 1152], P('narrow', 'wide'), may hold values from -1.5258789e-05 to 1.5258789e-05
- second_projections: float32 [8, 1152, 1152], P(None, 'wide', 'narrow'), may hold values from 7.2284855e-16 to 1.1565577e-14
- second_qkv_weights: float32 [2, 1152, 3456], P(None, 'wide', 'narrow'), may hold values from 7.2284855e-16 to 1.1565577e-14
- second_mlp_weights: float32 [2, 1152, 4608], P(None, 'wide', 'narrow'), may hold values from 7.2284855e-16 to 1.1565577e-14
- second_ada_weights: float32 [1152, 6912], P('wide', 'narrow'), may hold values from 7.2284855e-16 to 1.1565577e-14
- second_entry_weights: float32 [4352, 1152], P('wide', 'narrow'), may hold values from 7.2284855e-16 to 1.1565577e-14
- second_patch_weights: float32 [2, 1152, 16], P(None, 'wide', 'narrow'), may hold values from 7.2284855e-16 to 1.1565577e-14
- second_shift_tables: float32 [8, 1152], P('narrow', 'wide'), may hold values from 4.6262307e-14 to 7.401969e-13
- latents: bfloat16 [64, 256, 16], P(('wide', 'narrow')), may hold values from -6 to 6
- noise: bfloat16 [64, 256, 16], P(('wide', 'narrow')), may hold values from -6 to 6
- captions: bfloat16 [64, 120, 4096], P(('wide', 'narrow')), may hold values from -6 to 6
- cap_len: int32 [64], P(('wide', 'narrow')), may hold values from 5 to 120, as said below
- timesteps: int32 [64], P(('wide', 'narrow')), may hold values from 0 to 999
- step_count: int32 [1], replicated, may hold values from 2 to 20
Outputs:
- new_projections: float32 [8, 1152, 1152], P(None, 'wide', 'narrow')
- new_qkv_weights: float32 [2, 1152, 3456], P(None, 'wide', 'narrow')
- new_mlp_weights: float32 [2, 1152, 4608], P(None, 'wide', 'narrow')
- new_ada_weights: float32 [1152, 6912], P('wide', 'narrow')
- new_entry_weights: float32 [4352, 1152], P('wide', 'narrow')
- new_patch_weights: float32 [2, 1152, 16], P(None, 'wide', 'narrow')
- new_shift_tables: float32 [8, 1152], P('narrow', 'wide')
- new_first_projections: float32 [8, 1152, 1152], P(None, 'wide', 'narrow')
- new_first_qkv_weights: float32 [2, 1152, 3456], P(None, 'wide', 'narrow')
- new_first_mlp_weights: float32 [2, 1152, 4608], P(None, 'wide', 'narrow')
- new_first_ada_weights: float32 [1152, 6912], P('wide', 'narrow')
- new_first_entry_weights: float32 [4352, 1152], P('wide', 'narrow')
- new_first_patch_weights: float32 [2, 1152, 16], P(None, 'wide', 'narrow')
- new_first_shift_tables: float32 [8, 1152], P('narrow', 'wide')
- new_second_projections: float32 [8, 1152, 1152], P(None, 'wide', 'narrow')
- new_second_qkv_weights: float32 [2, 1152, 3456], P(None, 'wide', 'narrow')
- new_second_mlp_weights: float32 [2, 1152, 4608], P(None, 'wide', 'narrow')
- new_second_ada_weights: float32 [1152, 6912], P('wide', 'narrow')
- new_second_entry_weights: float32 [4352, 1152], P('wide', 'narrow')
- new_second_patch_weights: float32 [2, 1152, 16], P(None, 'wide', 'narrow')
- new_second_shift_tables: float32 [8, 1152], P('narrow', 'wide')
- loss: float32 [], replicated
- grad_norm: float32 [], replicated
The draws below stay inside these ranges and needn't reach their ends.
Inputs may be any that keep to these rules, and one draw needn't show every extreme that they name: `cap_len`: clip 0 has all 120 caption tokens.
All inputs are finite; a program needn't handle non-finite values.
Results may differ from the reference program's by a relative error of at most 0.0058.
Values may be sent and summed in bfloat16 or wider, within the bound.
No kernel may reach another device: no remote copies, remote signals or barrier semaphores. Data moves between devices by JAX's collectives and lax.ppermute only.
A program may use at most 576 MiB of HBM per device.

```python
import math
import jax
import jax.numpy as jnp
from jax import lax

D = 1152
HEADS = 16
HEAD_DIM = 72
FF = 4608
CAP = 4096
FREQ = 256
P_SIZE = 16
F = 16
S = 16
LCAP = 120
TOK = 256
VIDEOS = 64
NPARAM = 42218496


def draw_cap_len(key, part):
    lengths = jax.random.randint(key, (VIDEOS,), min(5, LCAP), LCAP + 1)
    return lengths.at[0].set(LCAP)


def draw_patch_weights(key, part):
    embed_part = jnp.clip(jax.random.normal(jax.random.fold_in(key, 11), (D, P_SIZE), jnp.float32), -6.0, 6.0) * P_SIZE ** (-0.5)
    final_part = jnp.clip(jax.random.normal(jax.random.fold_in(key, 12), (D, P_SIZE), jnp.float32), -6.0, 6.0) * D ** (-0.5)
    return jnp.stack([embed_part, final_part])


def plant(drawn, stream_key, smallest, largest):
    shape = drawn.shape
    index_at = [jax.random.randint(jax.random.fold_in(stream_key, axis), (), 0, shape[axis]) for axis in range(len(shape))]
    drawn = drawn.at[tuple(index_at)].set(smallest)
    longest = shape.index(max(shape))
    index_at[longest] = (index_at[longest] + 1) % shape[longest]
    return drawn.at[tuple(index_at)].set(largest)


def level_of(own_key, shape, shards, low, high):
    factor_of = 1.0
    for axis_at, shards_of in shards:
        draws = jax.random.uniform(jax.random.fold_in(jax.random.fold_in(own_key, 6), axis_at), (shards_of,), jnp.float32, low / len(shards), high / len(shards))
        factor_of = factor_of * jnp.repeat(jnp.exp(draws), shape[axis_at] // shards_of).reshape((-1,) + (1,) * (len(shape) - 1 - axis_at))
    return factor_of


def scatter_about(stream_key, shape, width, limit, shards=(), held_as=jnp.bfloat16):
    level = level_of(stream_key, shape, shards, -0.22, 0.18) if shards else 1.0
    entries = jax.random.normal(stream_key, shape, jnp.float32) * width * level
    return jnp.minimum(jnp.maximum(entries, -limit), limit).astype(held_as)


def setup_inputs(seed: int = 0) -> dict:
    key_list = jax.random.split(jax.random.key(seed), 28)
    return {
        "projections": scatter_about(key_list[0], (8, D, D), D ** -0.5, 0.1875, ((1, 16), (2, 2)), jnp.float32),
        "qkv_weights": scatter_about(key_list[1], (2, D, 3 * D), D ** -0.5, 0.1875, ((1, 16), (2, 2)), jnp.float32),
        "mlp_weights": scatter_about(key_list[2], (2, D, FF), D ** -0.5, 0.1875, ((1, 16), (2, 2)), jnp.float32),
        "ada_weights": scatter_about(key_list[3], (D, 6 * D), D ** -0.5, 0.1875, ((0, 16), (1, 2)), jnp.float32),
        "entry_weights": scatter_about(key_list[4], (CAP + FREQ, D), CAP ** -0.5, 0.09375, ((0, 16), (1, 2)), jnp.float32),
        "patch_weights": draw_patch_weights(jax.random.fold_in(key_list[27], 71), 0),
        "shift_tables": scatter_about(key_list[6], (8, D), 0.1, 0.5, ((0, 2), (1, 16)), jnp.float32),
        "first_projections": scatter_about(key_list[7], (8, D, D), (0.111 * (VIDEOS * TOK * NPARAM) ** -0.5), 1.9073486328125e-06, ((1, 16), (2, 2)), jnp.float32),
        "first_qkv_weights": scatter_about(key_list[8], (2, D, 3 * D), (0.111 * (VIDEOS * TOK * NPARAM) ** -0.5), 1.9073486328125e-06, ((1, 16), (2, 2)), jnp.float32),
        "first_mlp_weights": scatter_about(key_list[9], (2, D, FF), (0.111 * (VIDEOS * TOK * NPARAM) ** -0.5), 1.9073486328125e-06, ((1, 16), (2, 2)), jnp.float32),
        "first_ada_weights": scatter_about(key_list[10], (D, 6 * D), (0.111 * (VIDEOS * TOK * NPARAM) ** -0.5), 1.9073486328125e-06, ((0, 16), (1, 2)), jnp.float32),
        "first_entry_weights": scatter_about(key_list[11], (CAP + FREQ, D), (0.111 * (VIDEOS * TOK * NPARAM) ** -0.5), 1.9073486328125e-06, ((0, 16), (1, 2)), jnp.float32),
        "first_patch_weights": scatter_about(key_list[12], (2, D, P_SIZE), (0.111 * (VIDEOS * TOK * NPARAM) ** -0.5), 1.9073486328125e-06, ((1, 16), (2, 2)), jnp.float32),
        "first_shift_tables": scatter_about(key_list[13], (8, D), (0.9 * (VIDEOS * TOK * NPARAM) ** -0.5), 1.52587890625e-05, ((0, 2), (1, 16)), jnp.float32),
        "second_projections": jnp.clip(jnp.exp(math.log(1.1565576750157455e-14) - 2.7725887 * jax.random.uniform(key_list[14], (8, D, D), jnp.float32) ** level_of(key_list[14], (8, D, D), ((1, 16), (2, 2)), -0.2, 0.2)), 7.228485468848409e-16, 1.1565576750157455e-14),
        "second_qkv_weights": jnp.clip(jnp.exp(math.log(1.1565576750157455e-14) - 2.7725887 * jax.random.uniform(key_list[15], (2, D, 3 * D), jnp.float32) ** level_of(key_list[15], (2, D, 3 * D), ((1, 16), (2, 2)), -0.2, 0.2)), 7.228485468848409e-16, 1.1565576750157455e-14),
        "second_mlp_weights": jnp.clip(jnp.exp(math.log(1.1565576750157455e-14) - 2.7725887 * jax.random.uniform(key_list[16], (2, D, FF), jnp.float32) ** level_of(key_list[16], (2, D, FF), ((1, 16), (2, 2)), -0.2, 0.2)), 7.228485468848409e-16, 1.1565576750157455e-14),
        "second_ada_weights": jnp.clip(jnp.exp(math.log(1.1565576750157455e-14) - 2.7725887 * jax.random.uniform(key_list[17], (D, 6 * D), jnp.float32) ** level_of(key_list[17], (D, 6 * D), ((0, 16), (1, 2)), -0.2, 0.2)), 7.228485468848409e-16, 1.1565576750157455e-14),
        "second_entry_weights": jnp.clip(jnp.exp(math.log(1.1565576750157455e-14) - 2.7725887 * jax.random.uniform(key_list[18], (CAP + FREQ, D), jnp.float32) ** level_of(key_list[18], (CAP + FREQ, D), ((0, 16), (1, 2)), -0.2, 0.2)), 7.228485468848409e-16, 1.1565576750157455e-14),
        "second_patch_weights": jnp.clip(jnp.exp(math.log(1.1565576750157455e-14) - 2.7725887 * jax.random.uniform(key_list[19], (2, D, P_SIZE), jnp.float32) ** level_of(key_list[19], (2, D, P_SIZE), ((1, 16), (2, 2)), -0.2, 0.2)), 7.228485468848409e-16, 1.1565576750157455e-14),
        "second_shift_tables": jnp.clip(jnp.exp(math.log(7.401969120100771e-13) - 2.7725887 * jax.random.uniform(key_list[20], (8, D), jnp.float32) ** level_of(key_list[20], (8, D), ((0, 2), (1, 16)), -0.2, 0.2)), 4.626230700062982e-14, 7.401969120100771e-13),
        "latents": scatter_about(key_list[21], (VIDEOS, TOK, P_SIZE), 1.0, 6.0, ((0, 32),)),
        "noise": scatter_about(key_list[22], (VIDEOS, TOK, P_SIZE), 1.0, 6.0, ((0, 32),)),
        "captions": scatter_about(key_list[23], (VIDEOS, LCAP, CAP), 1.0, 6.0, ((0, 32),)),
        "cap_len": draw_cap_len(jax.random.fold_in(key_list[27], 71), 0),
        "timesteps": plant(jax.random.randint(key_list[25], (VIDEOS,), 0, 1000), jax.random.fold_in(key_list[25], 1), 0, 999).astype(jnp.int32),
        "step_count": jax.random.randint(key_list[26], (1,), 2, 21).astype(jnp.int32),
    }


@jax.custom_vjp
def low(v):
    return lax.optimization_barrier(v.astype(jnp.bfloat16)).astype(jnp.float32)

@jax.custom_vjp
def low_back(v):
    return v

def low_keep(v):
    return (low(v), None)

def low_pass(kept, grad):
    return (grad,)

def back_keep(v):
    return (v, None)

def back_low(kept, grad):
    return (low(grad),)
low.defvjp(low_keep, low_pass)
low_back.defvjp(back_keep, back_low)
HIGHEST = lax.Precision.HIGHEST
LEARNING_RATE = 0.04

def product(operand, matrix):
    return low_back(jnp.dot(low(operand), matrix, precision=HIGHEST))

def sinusoid(places, feature):
    half_width = feature // 2
    freqs_row = jnp.exp(-math.log(10000.0) * jnp.arange(half_width, dtype=jnp.float32) / half_width)
    angles = places[:, None] * freqs_row[None, :]
    return jnp.concatenate([jnp.cos(angles), jnp.sin(angles)], axis=1)

def layer_norm(values):
    centred = values - lax.optimization_barrier(jnp.mean(values, axis=-1, keepdims=True))
    return centred * lax.rsqrt(lax.optimization_barrier(jnp.mean(centred * centred, axis=-1, keepdims=True)) + 1e-06)

def modulate(values, shift_row, scale_row):
    return layer_norm(values) * (1.0 + scale_row) + shift_row

def attend(queries, key_rows, value_rows, allowed):
    groups, row_count, feature = queries.shape
    key_count = key_rows.shape[1]
    query_heads = low(queries).reshape(groups, row_count, HEADS, HEAD_DIM)
    key_heads = low(key_rows).reshape(groups, key_count, HEADS, HEAD_DIM)
    value_heads = low(value_rows).reshape(groups, key_count, HEADS, HEAD_DIM)
    scores = low_back(jnp.einsum('bnhd,bmhd->bhnm', query_heads, key_heads, precision=HIGHEST)) * HEAD_DIM ** (-0.5)
    if allowed is not None:
        scores = jnp.where(allowed, scores, -1000000000.0)
    attention = jax.nn.softmax(scores, axis=-1)
    mixture = jnp.einsum('bhnm,bmhd->bnhd', low(attention), value_heads, precision=HIGHEST)
    return low_back(mixture).reshape(groups, row_count, feature)

def video_loss(params, latent, noise_row, caption, length, timestep):
    projections, qkv_weights, mlp_weights, ada_weights, entry_weights, patch_weights, shift_tables = params
    time_value = timestep.astype(jnp.float32)
    signal = jnp.cos((time_value / 1000.0 + 0.008) / 1.008 * (math.pi / 2)) ** 2
    noised = jnp.sqrt(signal) * latent + jnp.sqrt(1.0 - signal) * noise_row
    spatial_pos = jnp.tile(sinusoid(jnp.arange(S, dtype=jnp.float32), D), (F, 1))
    frame_pos = sinusoid(jnp.arange(F, dtype=jnp.float32), D)
    hidden = product(noised, patch_weights[0].T) + spatial_pos
    time_inner = product(sinusoid(time_value.reshape(1), FREQ), entry_weights[CAP:])
    time_embed = product(jax.nn.silu(time_inner), projections[0])
    modulations = product(jax.nn.silu(time_embed), ada_weights).reshape(6, D) + shift_tables[:6]
    context = product(jax.nn.gelu(product(caption, entry_weights[:CAP])), projections[1])
    spatial_qkv = product(modulate(hidden, modulations[0], modulations[1]), qkv_weights[0]).reshape(F, S, 3 * D)
    spatial_mix = attend(spatial_qkv[..., :D], spatial_qkv[..., D:2 * D], spatial_qkv[..., 2 * D:], None)
    hidden = hidden + modulations[2] * product(spatial_mix.reshape(F * S, D), projections[2])
    temporal_in = (hidden.reshape(F, S, D) + frame_pos[:, None, :]).reshape(F * S, D)
    temporal_qkv = product(temporal_in, qkv_weights[1]).reshape(F, S, 3 * D).transpose(1, 0, 2)
    temporal_mix = attend(temporal_qkv[..., :D], temporal_qkv[..., D:2 * D], temporal_qkv[..., 2 * D:], None)
    temporal_mix = temporal_mix.transpose(1, 0, 2).reshape(F * S, D)
    hidden = hidden + modulations[2] * product(temporal_mix, projections[3])
    cross_query = product(hidden, projections[4])
    cross_pairs = product(context, jnp.concatenate([projections[5], projections[6]], axis=1))
    allowed = (jnp.arange(LCAP) < length)[None, None, None, :]
    cross_mix = attend(cross_query[None], cross_pairs[None, :, :D], cross_pairs[None, :, D:], allowed)[0]
    hidden = hidden + product(cross_mix, projections[7])
    mlp_inner = jax.nn.gelu(product(modulate(hidden, modulations[3], modulations[4]), mlp_weights[0]))
    hidden = hidden + modulations[5] * product(mlp_inner, mlp_weights[1].T)
    final_in = modulate(hidden, time_embed[0] + shift_tables[6], time_embed[0] + shift_tables[7])
    predicted = product(final_in, patch_weights[1])
    misfit = predicted - noise_row
    return jnp.mean(misfit * misfit)

def adam_update(master, first_moment, second_moment, gradient, step_value):
    first_new = 0.9 * first_moment + 0.1 * gradient
    second_new = 0.999 * second_moment + 0.001 * gradient * gradient
    first_hat = first_new / (1.0 - 0.9 ** step_value)
    second_hat = second_new / (1.0 - 0.999 ** step_value)
    master_new = master - LEARNING_RATE * (first_hat / (jnp.sqrt(second_hat) + 1e-08) + 0.01 * master)
    return (master_new, first_new, second_new)

def reference(projections, qkv_weights, mlp_weights, ada_weights, entry_weights, patch_weights, shift_tables, first_projections, first_qkv_weights, first_mlp_weights, first_ada_weights, first_entry_weights, first_patch_weights, first_shift_tables, second_projections, second_qkv_weights, second_mlp_weights, second_ada_weights, second_entry_weights, second_patch_weights, second_shift_tables, latents, noise, captions, cap_len, timesteps, step_count):
    masters = (projections, qkv_weights, mlp_weights, ada_weights, entry_weights, patch_weights, shift_tables)
    firsts = (first_projections, first_qkv_weights, first_mlp_weights, first_ada_weights, first_entry_weights, first_patch_weights, first_shift_tables)
    seconds = (second_projections, second_qkv_weights, second_mlp_weights, second_ada_weights, second_entry_weights, second_patch_weights, second_shift_tables)

    def video_term(parameters, sample):
        latent, noise_row, caption, length, timestep = sample
        lowered = tuple((low(parameter) for parameter in parameters))
        return video_loss(lowered, latent.astype(jnp.float32), noise_row.astype(jnp.float32), caption.astype(jnp.float32), length, timestep) / VIDEOS

    def accumulate(state_pair, sample):
        loss_value, pullback = jax.vjp(lambda parameters: video_term(parameters, sample), masters)
        gradients, = pullback(jnp.ones((), jnp.float32))
        running, summed = state_pair
        return ((running + loss_value, tuple((left_part + right_part for left_part, right_part in zip(summed, gradients)))), None)
    initial = (jnp.zeros((), jnp.float32), tuple((jnp.zeros_like(master) for master in masters)))
    (loss_total, summed), _ = lax.scan(accumulate, initial, (latents, noise, captions, cap_len, timesteps))
    grad_norm = jnp.sqrt(sum((jnp.sum(gradient * gradient) for gradient in summed)))
    threshold = (VIDEOS * F * S) ** (-0.5)
    factor = threshold / jnp.maximum(grad_norm, threshold)
    step_value = step_count[0].astype(jnp.float32)
    updated = [adam_update(master, first_moment, second_moment, gradient * factor, step_value) for master, first_moment, second_moment, gradient in zip(masters, firsts, seconds, summed)]
    return (updated[0][0], updated[1][0], updated[2][0], updated[3][0], updated[4][0], updated[5][0], updated[6][0], updated[0][1], updated[1][1], updated[2][1], updated[3][1], updated[4][1], updated[5][1], updated[6][1], updated[0][2], updated[1][2], updated[2][2], updated[3][2], updated[4][2], updated[5][2], updated[6][2], loss_total, grad_norm)
```

```python
import math

import jax
import jax.numpy as jnp
from jax import lax
from jax.experimental import pallas as pl
from jax.experimental.pallas import tpu as pltpu
from jax.sharding import PartitionSpec as P

D = 1152
HEADS = 16
HEAD_DIM = 72
CAP = 4096
FREQ = 256
F = 16
S = 16
LCAP = 120


LEARNING_RATE = 0.04


def rounded(values):
    return values.astype(jnp.bfloat16)


def matmul(operand, matrix):
    return jnp.dot(operand, matrix, preferred_element_type=jnp.float32)


def matmul_tn(operand, matrix):
    return lax.dot_general(
        operand, matrix, (((0,), (0,)), ((), ())), preferred_element_type=jnp.float32
    )


def matmul_nt(operand, matrix):
    return lax.dot_general(
        operand, matrix, (((1,), (1,)), ((), ())), preferred_element_type=jnp.float32
    )


def sinusoid(places, feature):
    half_width = feature // 2
    freqs_row = jnp.exp(-math.log(10000.0) * jnp.arange(half_width, dtype=jnp.float32) / half_width)
    angles = places[:, None] * freqs_row[None, :]
    return jnp.concatenate([jnp.cos(angles), jnp.sin(angles)], axis=1)


def layer_norm(values):
    centred = values - jnp.mean(values, axis=-1, keepdims=True)
    return centred * lax.rsqrt(jnp.mean(centred * centred, axis=-1, keepdims=True) + 1e-06)


def modulate(values, shift_row, scale_row):
    return layer_norm(values) * (1.0 + scale_row) + shift_row


def head_window(head):
    first = HEAD_DIM * head
    low_lane = first // 128 * 128
    high_lane = -(-(first + HEAD_DIM) // 128) * 128
    return (first - low_lane, low_lane, high_lane)


def lanes_of_head(rows, head):
    offset, low_lane, high_lane = head_window(head)
    lane = lax.broadcasted_iota(jnp.int32, (rows, high_lane - low_lane), 1)
    return (lane >= offset) & (lane < offset + HEAD_DIM)


def dot_f32(left, right, contract):
    return lax.dot_general(
        left, right, ((contract[:1], contract[1:]), ((), ())), preferred_element_type=jnp.float32
    )


def softmax_rows(scores, allowed):
    scores = jnp.where(allowed, scores * HEAD_DIM ** (-0.5), -1000000000.0)
    powers = jnp.exp(scores - jnp.max(scores, axis=-1, keepdims=True))
    return powers * (1.0 / jnp.sum(powers, axis=-1, keepdims=True))


def put_head(ref, base, head, window, values):
    _, low_lane, high_lane = window
    spot = (slice(None), slice(base + low_lane, base + high_lane))
    kept = ref[spot]
    mine = lanes_of_head(kept.shape[0], head)
    ref[spot] = jnp.where(mine, values, kept.astype(jnp.float32)).astype(ref.dtype)


def attend_heads(query_ref, key_ref, key_base, value_ref, value_base, out_ref, allowed):
    rows = query_ref.shape[0]
    for head in range(HEADS):
        window = head_window(head)
        _, low_lane, high_lane = window
        query = query_ref[:, low_lane:high_lane]
        query = jnp.where(lanes_of_head(rows, head), query, jnp.zeros_like(query))
        key = key_ref[:, key_base + low_lane : key_base + high_lane]
        weights = softmax_rows(dot_f32(query, key, (1, 1)), allowed)
        value = value_ref[:, value_base + low_lane : value_base + high_lane]
        put_head(out_ref, 0, head, window, dot_f32(rounded(weights), value, (1, 0)))


def attend_heads_back(
    query_ref, key_ref, key_base, value_ref, value_base, grad_ref,
    grad_query_ref, grad_key_ref, grad_value_ref, allowed,
):
    rows = query_ref.shape[0]
    for head in range(HEADS):
        window = head_window(head)
        _, low_lane, high_lane = window
        mine = lanes_of_head(rows, head)
        query = query_ref[:, low_lane:high_lane]
        zero = jnp.zeros_like(query)
        key = key_ref[:, key_base + low_lane : key_base + high_lane]
        value = value_ref[:, value_base + low_lane : value_base + high_lane]
        grad = grad_ref[:, low_lane:high_lane]
        weights = softmax_rows(dot_f32(jnp.where(mine, query, zero), key, (1, 1)), allowed)
        grad_weights = dot_f32(jnp.where(mine, grad, zero), value, (1, 1))
        put_head(grad_value_ref, value_base, head, window, dot_f32(rounded(weights), grad, (0, 0)))
        grad_scores = weights * (
            grad_weights - jnp.sum(grad_weights * weights, axis=-1, keepdims=True)
        )
        grad_low = rounded(grad_scores * HEAD_DIM ** (-0.5))
        put_head(grad_query_ref, 0, head, window, dot_f32(grad_low, key, (1, 0)))
        put_head(grad_key_ref, key_base, head, window, dot_f32(grad_low, query, (0, 0)))


def same_group(rows, spatial):
    row = lax.broadcasted_iota(jnp.int32, (rows, rows), 0)
    column = lax.broadcasted_iota(jnp.int32, (rows, rows), 1)
    if spatial:
        return row // S == column // S
    return row % S == column % S


VMEM_LIMIT = pltpu.CompilerParams(vmem_limit_bytes=48 * 1024 * 1024)


def self_attend(qkv, spatial):
    rows = F * S

    def kernel(qkv_ref, out_ref):
        out_ref[...] = jnp.zeros_like(out_ref)
        attend_heads(qkv_ref, qkv_ref, D, qkv_ref, 2 * D, out_ref, same_group(rows, spatial))

    return pl.pallas_call(
        kernel,
        grid=(qkv.shape[0] // rows,),
        in_specs=[pl.BlockSpec((rows, 3 * D), lambda i: (i, 0))],
        out_specs=pl.BlockSpec((rows, D), lambda i: (i, 0)),
        out_shape=jax.ShapeDtypeStruct((qkv.shape[0], D), jnp.bfloat16),
        compiler_params=VMEM_LIMIT,
        name="self_attend",
    )(qkv)


def self_attend_back(qkv, grad_mix, spatial):
    rows = F * S

    def kernel(qkv_ref, grad_ref, out_ref):
        out_ref[...] = jnp.zeros_like(out_ref)
        attend_heads_back(
            qkv_ref, qkv_ref, D, qkv_ref, 2 * D, grad_ref,
            out_ref, out_ref, out_ref, same_group(rows, spatial),
        )

    return pl.pallas_call(
        kernel,
        grid=(qkv.shape[0] // rows,),
        in_specs=[
            pl.BlockSpec((rows, 3 * D), lambda i: (i, 0)),
            pl.BlockSpec((rows, D), lambda i: (i, 0)),
        ],
        out_specs=pl.BlockSpec((rows, 3 * D), lambda i: (i, 0)),
        out_shape=jax.ShapeDtypeStruct(qkv.shape, jnp.bfloat16),
        compiler_params=VMEM_LIMIT,
        name="self_attend_back",
    )(qkv, grad_mix)


def caption_mask(length):
    return lax.broadcasted_iota(jnp.int32, (F * S, LCAP), 1) < length


def cross_attend(query, pairs, lengths):
    clips = pairs.shape[0]

    def kernel(length_ref, query_ref, pair_ref, out_ref):
        out_ref[...] = jnp.zeros_like(out_ref)
        allowed = caption_mask(length_ref[pl.program_id(0)])
        attend_heads(query_ref, pair_ref.at[0], 0, pair_ref.at[0], D, out_ref, allowed)

    return pl.pallas_call(
        kernel,
        grid_spec=pltpu.PrefetchScalarGridSpec(
            num_scalar_prefetch=1,
            grid=(clips,),
            in_specs=[
                pl.BlockSpec((F * S, D), lambda i, lens: (i, 0)),
                pl.BlockSpec((1, LCAP, 2 * D), lambda i, lens: (i, 0, 0)),
            ],
            out_specs=pl.BlockSpec((F * S, D), lambda i, lens: (i, 0)),
        ),
        out_shape=jax.ShapeDtypeStruct(query.shape, jnp.bfloat16),
        compiler_params=VMEM_LIMIT,
        name="cross_attend",
    )(lengths, query, pairs)


def cross_attend_back(query, pairs, grad_mix, lengths):
    clips = pairs.shape[0]

    def kernel(length_ref, query_ref, pair_ref, grad_ref, grad_query_ref, grad_pair_ref):
        grad_query_ref[...] = jnp.zeros_like(grad_query_ref)
        grad_pair_ref[...] = jnp.zeros_like(grad_pair_ref)
        allowed = caption_mask(length_ref[pl.program_id(0)])
        attend_heads_back(
            query_ref, pair_ref.at[0], 0, pair_ref.at[0], D, grad_ref,
            grad_query_ref, grad_pair_ref.at[0], grad_pair_ref.at[0], allowed,
        )

    return pl.pallas_call(
        kernel,
        grid_spec=pltpu.PrefetchScalarGridSpec(
            num_scalar_prefetch=1,
            grid=(clips,),
            in_specs=[
                pl.BlockSpec((F * S, D), lambda i, lens: (i, 0)),
                pl.BlockSpec((1, LCAP, 2 * D), lambda i, lens: (i, 0, 0)),
                pl.BlockSpec((F * S, D), lambda i, lens: (i, 0)),
            ],
            out_specs=[
                pl.BlockSpec((F * S, D), lambda i, lens: (i, 0)),
                pl.BlockSpec((1, LCAP, 2 * D), lambda i, lens: (i, 0, 0)),
            ],
        ),
        out_shape=[
            jax.ShapeDtypeStruct(query.shape, jnp.bfloat16),
            jax.ShapeDtypeStruct(pairs.shape, jnp.bfloat16),
        ],
        compiler_params=VMEM_LIMIT,
        name="cross_attend_back",
    )(lengths, query, pairs, grad_mix)


class Place:
    def __init__(self):
        self.wide = lax.axis_size("wide")
        self.narrow = lax.axis_size("narrow")
        self.depth = self.wide // 4
        self.half = self.depth // 2
        self.at = lax.axis_index("wide")
        self.core = self.at & 1
        self.x = (self.at >> 1) & 1
        self.z = self.at >> 2
        self.y = lax.axis_index("narrow")

    def over_wide(self, values, bit):
        return lax.ppermute(values, "wide", [(i, i ^ bit) for i in range(self.wide)])

    def over_core(self, values):
        return self.over_wide(values, 1)

    def over_x(self, values):
        return self.over_wide(values, 2)

    def over_z(self, values, bit):
        return self.over_wide(values, 4 * bit)

    def to_owner(self, values):
        pairs = [
            (i, i ^ 4 * self.half)
            for i in range(self.wide)
            if (i >> 2) // self.half != i & 1
        ]
        return lax.ppermute(values, "wide", pairs)

    def from_owner(self, values):
        pairs = [(i, i ^ 1) for i in range(self.wide) if (i >> 2) // self.half == i & 1]
        return lax.ppermute(values, "wide", pairs)

    def over_y(self, values, bit):
        return lax.ppermute(values, "narrow", [(i, i ^ bit) for i in range(self.narrow)])


def pair_up(bit, own, other):
    first = bit == 0
    return jnp.where(first, own, other), jnp.where(first, other, own)


def bits_of(size):
    return [1 << at for at in range(size.bit_length() - 1)]


def hold(values, others):
    if not others:
        return values
    kept, _ = lax.optimization_barrier((values, others))
    return kept


class Ticks:
    def __init__(self, joint):
        self.joint = joint
        self.ended = {True: [], False: []}
        self.sent = []

    def run(self, jobs, others=()):
        self.before = self.ended[True]
        ended = {True: [], False: []}
        before = dict(self.ended)
        if self.joint:
            before = {kind: list(before.values()) for kind in before}
            self.ended = {True: [], False: []}
        self.sent = []
        results = []
        for kind in (True, False):
            mine = [job for job in jobs if job.planar == kind]
            if not mine:
                continue
            values = [[value for value, _ in job.sends] for job in mine]
            values = hold(values, [before[kind], list(others)])
            self.sent.append(values)
            for job, held in zip(mine, values):
                result = [exchange(value) for value, (_, exchange) in zip(held, job.sends)]
                ended[kind].append(result)
                results.append((job, result))
            self.ended[kind] = ended[kind]
        for job, result in results:
            job.take(result)

    def during(self, values):
        return hold(values, [self.sent, self.before])

    def after(self, values):
        return hold(values, self.ended[True])


class Job:
    planar = False

    def __init__(self, transfers):
        self.transfers = transfers
        self.sends = next(transfers)

    def take(self, results):
        try:
            self.sends = self.transfers.send(results)
        except StopIteration:
            self.sends = None


def spread_y(place, values):
    pieces = [values]
    for bit in bits_of(place.narrow):
        pieces = pieces + [place.over_y(piece, bit) for piece in pieces]
    return pieces[1:]


class Gather(Job):
    def __init__(self, place, own):
        self.place = place
        super().__init__(self.plan(own[None]))

    def plan(self, block):
        place = self.place
        half = place.half
        for bit in bits_of(half):
            [other] = yield [(block, lambda values, bit=bit: place.over_z(values, bit))]
            block = jnp.concatenate(pair_up(place.z & bit, block, other))
        quarter = half // 2
        low, high = block[:quarter], block[quarter:]
        [low_away] = yield [(low, lambda values: place.over_z(values, half))]
        [high_away] = yield [(high, lambda values: place.over_z(values, half))]
        low = pair_up(place.z & half, low, low_away)
        high = pair_up(place.z & half, high, high_away)
        block = jnp.concatenate([low[0], high[0], low[1], high[1]])
        self.planar = True
        by_x, by_y = yield [(block, place.over_x), (block, lambda values: spread_y(place, values))]
        far_xy, near_xy = yield [
            (jnp.stack([piece[half:] for piece in by_y]), place.over_x),
            (by_x[:half], lambda values: spread_y(place, values)),
        ]
        columns = block.shape[-1] * place.narrow
        mine = unwritten((place.depth, 2, block.shape[1], columns))
        parts = (
            (0, 0, self.lanes([block] + list(by_y))),
            (0, 1, self.lanes([by_x[:half]] + list(near_xy))),
            (half, 1, self.lanes([by_x[half:]] + [far_xy[at] for at in range(place.narrow - 1)])),
        )
        for first_z, apart, part in parts:
            mine = lax.dynamic_update_slice(
                mine, part[:, None], (first_z, place.x ^ apart, 0, 0)
            )
        self.mine = mine
        self.planar = False
        [self.other] = yield [(mine, place.over_core)]

    def lanes(self, pieces):
        place = self.place
        if place.narrow == 1:
            return pieces[0]
        if place.narrow == 2:
            return jnp.concatenate(pair_up(place.y, pieces[0], pieces[1]), axis=-1)
        return jnp.concatenate(
            [lax.select_n(place.y ^ spot, *pieces) for spot in range(place.narrow)], axis=-1
        )

    def whole(self, first_row, rows):
        place = self.place
        span = slice(first_row, first_row + rows)
        columns = self.mine.shape[-1]
        whole = unwritten((place.depth, 2, 2, rows, columns))
        for part, core in ((self.mine, place.core), (self.other, 1 - place.core)):
            whole = lax.dynamic_update_slice(
                whole, part[:, :, None, span], (0, 0, core, 0, 0)
            )
        return whole.reshape(place.wide * rows, columns)


def unwritten(shape):
    return pl.pallas_call(
        lambda out_ref: None,
        out_specs=pl.BlockSpec(memory_space=pl.ANY),
        out_shape=jax.ShapeDtypeStruct(shape, jnp.bfloat16),
        name="unwritten",
    )()


def side(values, bit, axis):
    return lax.dynamic_index_in_dim(values, bit, axis, keepdims=False)


def columns_at(values, index, count):
    width = values.shape[-1] // count
    if count == 1:
        return values
    if count == 2:
        return jnp.where(index == 0, values[..., :width], values[..., width:])
    return lax.dynamic_slice_in_dim(values, index * width, width, axis=values.ndim - 1)


def wide_float(values):
    return values.astype(jnp.float32)


def reduce_y(place, values):
    for bit in reversed(bits_of(place.narrow)):
        upper = ((place.y & bit) != 0).astype(jnp.int32)
        away = place.over_y(rounded(columns_at(values, 1 - upper, 2)), bit)
        values = columns_at(values, upper, 2) + wide_float(away)
    return values


class Scatter(Job):
    def __init__(self, place, products):
        self.place = place
        super().__init__(self.plan(products))

    def plan(self, products):
        place = self.place
        spread = place.half
        quarter = spread // 2
        sends = []
        for operand, grad, *known in products:
            sends.append((columns_at(operand, 1 - place.core, 2), place.over_core))
            if not known:
                sends.append((grad, place.over_core))
        away = iter((yield sends))
        sums = []
        for operand, grad, *known in products:
            kept = rounded(matmul_tn(columns_at(operand, place.core, 2), grad))
            operand_away = next(away)
            grad_away = known[0] if known else next(away)
            total = matmul_tn(operand_away, grad_away) + wide_float(kept)
            sums.append(rounded(total).reshape(spread, 2, -1, grad.shape[1]))
        rows = sums[0].shape[2] // 2

        def summed(span, x_bit=None):
            mine = [view[span] for view in sums]
            if x_bit is not None:
                mine = [side(view, x_bit, 1) for view in mine]
            return jnp.stack(mine)

        near_span, far_span = slice(0, quarter), slice(quarter, None)
        self.planar = True
        if place.narrow == 2:
            near_away, far_away = yield [
                (summed(near_span, 1 - place.x), place.over_x),
                (
                    jnp.stack([columns_at(view[far_span], 1 - place.y, 2) for view in sums]),
                    lambda values: place.over_y(values, 1),
                ),
            ]

            def near(y_bit):
                mine = [columns_at(side(view[near_span], place.x, 1), y_bit, 2) for view in sums]
                return wide_float(jnp.stack(mine)) + wide_float(columns_at(near_away, y_bit, 2))

            def far(x_bit):
                mine = [columns_at(side(view[far_span], x_bit, 1), place.y, 2) for view in sums]
                return wide_float(jnp.stack(mine)) + wide_float(side(far_away, x_bit, 2))

            near_back, far_back = yield [
                (rounded(near(1 - place.y)), lambda values: place.over_y(values, 1)),
                (rounded(far(1 - place.x)), place.over_x),
            ]
            near = near(place.y) + wide_float(near_back)
            far = far(place.x) + wide_float(far_back)
        else:
            near_away, far = yield [
                (summed(near_span, 1 - place.x), place.over_x),
                (wide_float(summed(far_span)), lambda values: reduce_y(place, values)),
            ]
            near = wide_float(summed(near_span, place.x)) + wide_float(near_away)
            near, far_back = yield [
                (near, lambda values: reduce_y(place, values)),
                (rounded(side(far, 1 - place.x, 2)), place.over_x),
            ]
            far = side(far, place.x, 2) + wide_float(far_back)
        self.planar = False
        total, sent = pair_up(place.z & quarter, near, far)
        [away] = yield [(rounded(sent), lambda values: place.over_z(values, quarter))]
        total = total + wide_float(away)
        for bit in reversed(bits_of(quarter)):
            total = total.reshape((total.shape[0], 2, total.shape[1] // 2) + total.shape[2:])
            upper = ((place.z & bit) != 0).astype(jnp.int32)
            [away] = yield [
                (
                    rounded(side(total, 1 - upper, 1)),
                    lambda values, bit=bit: place.over_z(values, bit),
                )
            ]
            total = side(total, upper, 1) + wide_float(away)
        total = total[:, 0]
        [away] = yield [(rounded(total), place.to_owner)]
        total = total + wide_float(away)
        total = total.reshape(total.shape[0], 2, rows, -1)
        [away] = yield [(side(total, 1 - place.core, 1), place.from_owner)]
        owner = place.z // spread == place.core
        self.total = jnp.where(owner, side(total, place.core, 1), away)


class Reducer:
    def __init__(self, place):
        self.place = place
        self.ticks = Ticks(False)
        self.jobs = []

    def add(self, *products):
        job = Scatter(self.place, products)
        self.jobs.append(job)
        return job

    def run(self, *waiting):
        due = [job for job in self.jobs if job.sends is not None and job not in waiting]
        if due:
            self.ticks.run(due)
        return bool(due)


def all_bits(place):
    pairs = [
        (place.y & bit, lambda values, bit=bit: place.over_y(values, bit))
        for bit in bits_of(place.narrow)
    ]
    return pairs + wide_bits(place)


def wide_bits(place):
    return [
        (place.at & bit, lambda values, bit=bit: place.over_wide(values, bit))
        for bit in bits_of(place.wide)
    ]


def sum_everywhere(place, values):
    for _, exchange in all_bits(place):
        values = values + exchange(values)
    return values


def adam_update(master, first_moment, second_moment, gradient, step_value):
    first_new = 0.9 * first_moment + 0.1 * gradient
    second_new = 0.999 * second_moment + 0.001 * gradient * gradient
    first_hat = first_new / (1.0 - 0.9**step_value)
    second_hat = second_new / (1.0 - 0.999**step_value)
    master_new = master - LEARNING_RATE * (
        first_hat / (jnp.sqrt(second_hat) + 1e-08) + 0.01 * master
    )
    return (master_new, first_new, second_new)


def body(
    projections,
    qkv_weights,
    mlp_weights,
    ada_weights,
    entry_weights,
    patch_weights,
    shift_tables,
    first_projections,
    first_qkv_weights,
    first_mlp_weights,
    first_ada_weights,
    first_entry_weights,
    first_patch_weights,
    first_shift_tables,
    second_projections,
    second_qkv_weights,
    second_mlp_weights,
    second_ada_weights,
    second_entry_weights,
    second_patch_weights,
    second_shift_tables,
    latents,
    noise,
    captions,
    cap_len,
    timesteps,
    step_count,
):
    shards = (
        projections,
        qkv_weights,
        mlp_weights,
        ada_weights,
        entry_weights,
        patch_weights,
        shift_tables,
    )
    firsts = (
        first_projections,
        first_qkv_weights,
        first_mlp_weights,
        first_ada_weights,
        first_entry_weights,
        first_patch_weights,
        first_shift_tables,
    )
    seconds = (
        second_projections,
        second_qkv_weights,
        second_mlp_weights,
        second_ada_weights,
        second_entry_weights,
        second_patch_weights,
        second_shift_tables,
    )
    place = Place()
    clips = latents.shape[0]
    tokens = F * S
    video_count = clips * place.wide * place.narrow
    rows = projections.shape[1]
    entry_rows = entry_weights.shape[0]

    def by_clip(values):
        return values.reshape(clips, tokens, values.shape[-1])

    def flat(values):
        return values.reshape(clips * tokens, values.shape[-1])

    devices = place.wide * place.narrow
    all_clips = clips * devices

    def to_all(values):
        return lax.all_to_all(values, ("wide", "narrow"), split_axis=0, concat_axis=0, tiled=True)

    def columns_to_all(values):
        pieces = values.reshape(values.shape[0], place.narrow, -1).transpose(1, 0, 2)
        pieces = jnp.broadcast_to(pieces[None], (place.wide,) + pieces.shape)
        return to_all(pieces.reshape((devices,) + pieces.shape[2:]))

    proj_low, qkv_low, mlp_low, ada_low, entry_low, patch_low, table_low = (
        rounded(shard) for shard in shards
    )
    width = projections.shape[2]
    small = jnp.concatenate([patch_low.reshape(-1), table_low.reshape(-1)])
    small_rows = -(-small.shape[0] // (8 * width)) * 8
    small = jnp.pad(small, (0, small_rows * width - small.shape[0])).reshape(small_rows, width)
    ticks = Ticks(True)
    gathers = [
        Gather(place, own)
        for own in (
            jnp.concatenate([proj_low[:2].reshape(2 * rows, width), small]),
            entry_low,
            qkv_low.reshape(2 * rows, -1),
            proj_low[2:].reshape(6 * rows, width),
            mlp_low[0],
            mlp_low[1],
        )
    ]
    early, entry_gather, qkv_gather, late, mlp_in_gather, mlp_out_gather = gathers
    rounds = iter(range(2 * len(gathers) + len(bits_of(place.depth)) + 4))

    def gather_on(*others):
        now = next(rounds)
        due = [job for at, job in enumerate(gathers) if job.sends is not None and now >= 2 * at]
        if due:
            ticks.run(due, others)

    while entry_gather.sends is not None:
        gather_on()
    gather_on()
    entry_gather.other = ticks.during(entry_gather.other)
    small_all = early.whole(2 * rows, small_rows)
    proj_all = [early.whole(0, rows), early.whole(rows, rows)]
    entry_all = entry_gather.whole(0, entry_rows)
    small_all = small_all.reshape(place.wide, small_rows, place.narrow, width).transpose(0, 2, 1, 3)
    small_all = small_all.reshape(place.wide, place.narrow, small_rows * width)
    patch_count = patch_low.size
    patch_all = small_all[:, :, :patch_count].reshape(
        (place.wide, place.narrow) + patch_low.shape
    )
    patch_all = patch_all.transpose(2, 0, 3, 1, 4).reshape(2, D, -1)
    table_all = small_all[:, :, patch_count : patch_count + table_low.size].reshape(
        (place.wide, place.narrow) + table_low.shape
    )
    table_all = table_all.transpose(1, 2, 0, 3).reshape(8, D).astype(jnp.float32)

    time_value = timesteps.astype(jnp.float32)
    signal = jnp.cos((time_value / 1000.0 + 0.008) / 1.008 * (math.pi / 2)) ** 2
    noise_rows = flat(noise.astype(jnp.float32))
    noised_low = rounded(
        flat(
            jnp.sqrt(signal)[:, None, None] * latents.astype(jnp.float32)
            + jnp.sqrt(1.0 - signal)[:, None, None] * noise.astype(jnp.float32)
        )
    )
    spatial_pos = jnp.tile(sinusoid(jnp.arange(S, dtype=jnp.float32), D), (clips * F, 1))
    frame_pos = jnp.tile(jnp.repeat(sinusoid(jnp.arange(F, dtype=jnp.float32), D), S, 0), (clips, 1))
    embed_low = rounded(sinusoid(time_value, FREQ))
    time_inner = matmul(embed_low, entry_all[CAP:])
    inner_low = rounded(jax.nn.silu(time_inner))
    time_embed = matmul(inner_low, proj_all[0])
    embed_act = rounded(jax.nn.silu(time_embed))

    def by_rows(values):
        return values.reshape(clips, place.wide, rows).transpose(1, 0, 2)

    sent = jnp.concatenate(
        [
            by_rows(embed_act),
            by_rows(inner_low),
            jnp.broadcast_to(embed_low[None], (place.wide,) + embed_low.shape),
        ],
        axis=-1,
    )
    sent = jnp.broadcast_to(sent[:, None], (place.wide, place.narrow) + sent.shape[1:])
    sent = to_all(sent.reshape((devices,) + sent.shape[2:])).reshape(all_clips, -1)
    my_embed_act, my_inner, embed_all = sent[:, :rows], sent[:, rows : 2 * rows], sent[:, 2 * rows :]
    part = to_all(matmul(my_embed_act, ada_low).reshape(devices, clips, -1))
    part = part.reshape(place.wide, place.narrow, clips, -1)
    modulations = jnp.sum(part, axis=0).transpose(1, 0, 2).reshape(clips, 6, D) + table_all[:6]
    shift_a, scale_a, gate_a, shift_m, scale_m, gate_m = (
        modulations[:, at : at + 1] for at in range(6)
    )
    final_shift = (time_embed + table_all[6])[:, None]
    final_scale = (time_embed + table_all[7])[:, None]

    gather_on(entry_all)
    caption_rows = captions.reshape(clips * LCAP, CAP)
    caption_inner = matmul(caption_rows, entry_all[:CAP])
    caption_act = rounded(jax.nn.gelu(caption_inner))
    context_low = rounded(matmul(caption_act, proj_all[1]))
    gather_on(context_low, part)
    qkv_gather.other = ticks.during(qkv_gather.other)
    qkv_all = [qkv_gather.whole(0, rows), qkv_gather.whole(rows, rows)]
    gather_on(*qkv_all)

    hidden = matmul_nt(noised_low, patch_all[0]) + spatial_pos
    normed_spatial = rounded(flat(modulate(by_clip(hidden), shift_a, scale_a)))
    spatial_qkv = rounded(matmul(normed_spatial, qkv_all[0]))
    spatial_mix = self_attend(spatial_qkv, True)
    gather_on(spatial_mix)
    late.other = ticks.during(late.other)
    proj_all = proj_all + [late.whole(at * rows, rows) for at in range(6)]
    pair_weight = jnp.concatenate([proj_all[5], proj_all[6]], axis=1)
    gather_on(*proj_all)
    cross_pairs = rounded(matmul(ticks.during(context_low), pair_weight))
    spatial_out = matmul(spatial_mix, proj_all[2])
    hidden_one = hidden + flat(gate_a * by_clip(spatial_out))
    temporal_in = rounded(hidden_one + frame_pos)
    temporal_qkv = rounded(matmul(temporal_in, qkv_all[1]))
    temporal_mix = self_attend(temporal_qkv, False)
    gather_on(cross_pairs, temporal_mix)
    mlp_in_gather.other = ticks.during(mlp_in_gather.other)
    mlp_in = mlp_in_gather.whole(0, rows)
    temporal_out = matmul(temporal_mix, proj_all[3])
    hidden_two = hidden_one + flat(gate_a * by_clip(temporal_out))
    hidden_two_low = rounded(hidden_two)
    cross_query = rounded(matmul(hidden_two_low, proj_all[4]))
    while mlp_out_gather.sends is not None:
        gather_on(cross_query, mlp_in)
    mlp_out = mlp_out_gather.whole(0, rows)
    cross_mix = cross_attend(cross_query, cross_pairs.reshape(clips, LCAP, 2 * D), cap_len)
    hidden_three = hidden_two + matmul(cross_mix, proj_all[7])
    normed_mlp = rounded(flat(modulate(by_clip(hidden_three), shift_m, scale_m)))
    expand = matmul(normed_mlp, mlp_in)
    expand_act = rounded(jax.nn.gelu(expand))
    expand_act_away = place.over_core(expand_act)
    contract = matmul_nt(expand_act, mlp_out)
    hidden_four = hidden_three + flat(gate_m * by_clip(contract))
    final_low = rounded(flat(modulate(by_clip(hidden_four), final_shift, final_scale)))
    misfit = matmul(final_low, patch_all[1]) - noise_rows
    entries = tokens * latents.shape[2]
    loss_value = jnp.sum(misfit * misfit) / (entries * video_count)

    grad_pred = rounded(2.0 * misfit / (entries * video_count))
    grad_patch_out = matmul_tn(final_low, grad_pred)
    _, pull_final = jax.vjp(modulate, by_clip(hidden_four), final_shift, final_scale)
    grad_four, grad_fshift, grad_fscale = pull_final(by_clip(matmul_nt(grad_pred, patch_all[1])))
    grad_contract = rounded(flat(grad_four * gate_m))
    grad_gate_mlp = jnp.sum(grad_four * by_clip(contract), axis=1)
    reducer = Reducer(place)
    during, after = reducer.ticks.during, reducer.ticks.after
    mlp_out_scatter = reducer.add((grad_contract, expand_act, expand_act_away))
    reducer.run()
    reducer.run()
    _, pull_gelu = jax.vjp(jax.nn.gelu, expand)
    grad_expand = rounded(pull_gelu(matmul(during(grad_contract), mlp_out))[0])
    grad_expand = after(grad_expand)
    mlp_in_scatter = reducer.add((normed_mlp, grad_expand))
    reducer.run()
    _, pull_mlp_norm = jax.vjp(modulate, by_clip(hidden_three), shift_m, scale_m)
    grad_three_part, grad_shift_mlp, grad_scale_mlp = pull_mlp_norm(
        by_clip(matmul_nt(during(grad_expand), mlp_in))
    )
    grad_three = flat(grad_four + grad_three_part)
    grad_cross_out = after(rounded(grad_three))
    grad_cross_mix = rounded(matmul_nt(during(grad_cross_out), proj_all[7]))
    grad_cross_mix = after(grad_cross_mix)
    reducer.run()
    grad_query_low, grad_pairs_low = cross_attend_back(
        cross_query, cross_pairs.reshape(clips, LCAP, 2 * D), during(grad_cross_mix), cap_len
    )
    grad_query_low, grad_pairs_low = after((grad_query_low, grad_pairs_low))
    grad_pairs_low = grad_pairs_low.reshape(clips * LCAP, 2 * D)
    reducer.run()
    grad_two = grad_three + matmul_nt(during(grad_query_low), proj_all[4])
    grad_temporal_out = rounded(flat(by_clip(grad_two) * gate_a))
    grad_gate_attn = jnp.sum(by_clip(grad_two * temporal_out), axis=1)
    grad_temporal_mix = rounded(matmul_nt(grad_temporal_out, proj_all[3]))
    grad_temporal_qkv = self_attend_back(temporal_qkv, grad_temporal_mix, False)
    grad_temporal_qkv = after(grad_temporal_qkv)
    qkv_one_scatter = reducer.add((temporal_in, grad_temporal_qkv))
    reducer.run()
    grad_one = grad_two + matmul_nt(grad_temporal_qkv, qkv_all[1])
    grad_spatial_out = rounded(flat(by_clip(grad_one) * gate_a))
    grad_gate_attn = grad_gate_attn + jnp.sum(by_clip(grad_one * spatial_out), axis=1)
    grad_spatial_mix = rounded(matmul_nt(grad_spatial_out, proj_all[2]))
    reducer.run()
    grad_spatial_qkv = self_attend_back(spatial_qkv, during(grad_spatial_mix), True)
    grad_spatial_qkv = after(grad_spatial_qkv)
    qkv_zero_scatter = reducer.add((normed_spatial, grad_spatial_qkv))
    reducer.run()
    grad_normed_spatial = after(matmul_nt(during(grad_spatial_qkv), qkv_all[0]))
    reducer.run()
    qkv_zero_started = reducer.ticks.sent
    grad_context = rounded(matmul_nt(during(grad_pairs_low), pair_weight))
    square_scatter = reducer.add(
        (spatial_mix, grad_spatial_out),
        (temporal_mix, grad_temporal_out),
        (hidden_two_low, grad_query_low),
        (cross_mix, grad_cross_out),
    )
    reducer.run()
    reducer.run()
    _, pull_caption = jax.vjp(jax.nn.gelu, caption_inner)
    grad_caption_inner = rounded(pull_caption(matmul_nt(during(grad_context), proj_all[1]))[0])
    caption_wide = jnp.pad(caption_rows, ((0, 0), (0, place.wide * entry_rows - CAP)))
    entry_scatter = reducer.add((caption_wide, grad_caption_inner))
    reducer.run()
    reducer.run()
    caption_scatter = reducer.add(
        (caption_act, grad_context),
        (context_low, grad_pairs_low[:, :D]),
        (context_low, grad_pairs_low[:, D:]),
    )
    while reducer.run():
        pass
    sum_mlp_in, sum_mlp_out = mlp_in_scatter.total[0], mlp_out_scatter.total[0]
    sum_qkv_one = qkv_one_scatter.total[0]
    sum_qkv_zero = qkv_zero_scatter.total[0]
    sum_two, sum_three, sum_four, sum_seven = square_scatter.total
    sum_one, sum_five, sum_six = caption_scatter.total
    sum_entry = entry_scatter.total[0]
    _, pull_spatial_norm = jax.vjp(modulate, by_clip(hidden), shift_a, scale_a)
    grad_hidden_part, grad_shift_attn, grad_scale_attn = pull_spatial_norm(
        by_clip(grad_normed_spatial)
    )
    grad_hidden = rounded(grad_one + flat(grad_hidden_part))
    grad_patch_in = matmul_tn(grad_hidden, noised_low)
    grad_modulations = jnp.stack(
        [
            grad_shift_attn[:, 0],
            grad_scale_attn[:, 0],
            grad_gate_attn,
            grad_shift_mlp[:, 0],
            grad_scale_mlp[:, 0],
            grad_gate_mlp,
        ],
        axis=1,
    )

    grad_ada_out = hold(rounded(grad_modulations.reshape(clips, 6 * D)), qkv_zero_started)
    grad_ada_mine = columns_to_all(grad_ada_out).reshape(all_clips, -1)
    grad_ada = matmul_tn(my_embed_act, grad_ada_mine)
    act_part = to_all(matmul_nt(grad_ada_mine, ada_low).reshape(devices, clips, rows))
    act_part = jnp.sum(act_part.reshape(place.wide, place.narrow, clips, rows), axis=1)
    grad_embed_act = act_part.transpose(1, 0, 2).reshape(clips, D)
    _, pull_embed = jax.vjp(jax.nn.silu, time_embed)
    grad_time_embed = rounded(
        pull_embed(grad_embed_act)[0] + (grad_fshift + grad_fscale)[:, 0]
    )
    _, pull_inner = jax.vjp(jax.nn.silu, time_inner)
    grad_time_inner = rounded(pull_inner(matmul_nt(grad_time_embed, proj_all[0]))[0])
    time_rows = columns_to_all(jnp.concatenate([grad_time_embed, grad_time_inner]))
    grad_embed_mine = time_rows[:, :clips].reshape(all_clips, width)
    grad_inner_mine = time_rows[:, clips:].reshape(all_clips, width)
    grad_proj_zero = matmul_tn(my_inner, grad_embed_mine)
    grad_time_rows = matmul_tn(embed_all, grad_inner_mine)
    spot = jnp.clip((place.at + 1) * entry_rows - CAP, 0, FREQ + entry_rows)
    padded_rows = jnp.pad(grad_time_rows, ((entry_rows, entry_rows), (0, 0)))
    grad_entry_time = lax.dynamic_slice_in_dim(padded_rows, spot, entry_rows, axis=0)

    grad_tables = jnp.concatenate(
        [
            jnp.sum(grad_modulations, axis=0),
            jnp.sum(grad_fshift, axis=0),
            jnp.sum(grad_fscale, axis=0),
        ]
    )
    grad_patches = jnp.stack([grad_patch_in, grad_patch_out]).reshape(
        2, place.wide, rows, place.narrow, -1
    )
    grad_tables = grad_tables.reshape(place.narrow, -1, place.wide, rows)
    small_grads = jnp.concatenate(
        [
            grad_patches.transpose(1, 3, 0, 2, 4).reshape(devices, -1),
            grad_tables.transpose(2, 0, 1, 3).reshape(devices, -1),
        ],
        axis=1,
    )
    small_grads = jnp.sum(to_all(small_grads), axis=0)
    sum_patch = small_grads[: patch_weights.size].reshape(patch_weights.shape)
    sum_tables = small_grads[patch_weights.size :].reshape(shift_tables.shape)

    sum_projections = jnp.stack(
        [
            grad_proj_zero,
            sum_one,
            sum_two,
            sum_three,
            sum_four,
            sum_five,
            sum_six,
            sum_seven,
        ]
    )
    summed = (
        sum_projections,
        jnp.stack([sum_qkv_zero, sum_qkv_one]),
        jnp.stack([sum_mlp_in, sum_mlp_out]),
        grad_ada,
        sum_entry + grad_entry_time,
        sum_patch,
        sum_tables,
    )
    square_part = sum((jnp.sum(piece * piece) for piece in summed))
    both = jnp.stack([loss_value, square_part])[:, None] * jnp.ones((1, 128), jnp.float32)
    both = sum_everywhere(place, both)
    loss_total, square_total = both[0, 0], both[1, 0]
    grad_norm = jnp.sqrt(square_total)
    threshold = (video_count * latents.shape[1]) ** (-0.5)
    factor = threshold / jnp.maximum(grad_norm, threshold)
    step_value = step_count[0].astype(jnp.float32)
    updated = [
        adam_update(master, first_moment, second_moment, gradient * factor, step_value)
        for master, first_moment, second_moment, gradient in zip(shards, firsts, seconds, summed)
    ]
    return (
        updated[0][0],
        updated[1][0],
        updated[2][0],
        updated[3][0],
        updated[4][0],
        updated[5][0],
        updated[6][0],
        updated[0][1],
        updated[1][1],
        updated[2][1],
        updated[3][1],
        updated[4][1],
        updated[5][1],
        updated[6][1],
        updated[0][2],
        updated[1][2],
        updated[2][2],
        updated[3][2],
        updated[4][2],
        updated[5][2],
        updated[6][2],
        loss_total,
        grad_norm,
    )


def solution(mesh):
    return jax.shard_map(
        body,
        mesh=mesh,
        in_specs=(
            P(None, "wide", "narrow"),
            P(None, "wide", "narrow"),
            P(None, "wide", "narrow"),
            P("wide", "narrow"),
            P("wide", "narrow"),
            P(None, "wide", "narrow"),
            P("narrow", "wide"),
            P(None, "wide", "narrow"),
            P(None, "wide", "narrow"),
            P(None, "wide", "narrow"),
            P("wide", "narrow"),
            P("wide", "narrow"),
            P(None, "wide", "narrow"),
            P("narrow", "wide"),
            P(None, "wide", "narrow"),
            P(None, "wide", "narrow"),
            P(None, "wide", "narrow"),
            P("wide", "narrow"),
            P("wide", "narrow"),
            P(None, "wide", "narrow"),
            P("narrow", "wide"),
            P(("wide", "narrow"), None, None),
            P(("wide", "narrow"), None, None),
            P(("wide", "narrow"), None, None),
            P(("wide", "narrow")),
            P(("wide", "narrow")),
            P(),
        ),
        out_specs=(
            P(None, "wide", "narrow"),
            P(None, "wide", "narrow"),
            P(None, "wide", "narrow"),
            P("wide", "narrow"),
            P("wide", "narrow"),
            P(None, "wide", "narrow"),
            P("narrow", "wide"),
            P(None, "wide", "narrow"),
            P(None, "wide", "narrow"),
            P(None, "wide", "narrow"),
            P("wide", "narrow"),
            P("wide", "narrow"),
            P(None, "wide", "narrow"),
            P("narrow", "wide"),
            P(None, "wide", "narrow"),
            P(None, "wide", "narrow"),
            P(None, "wide", "narrow"),
            P("wide", "narrow"),
            P("wide", "narrow"),
            P(None, "wide", "narrow"),
            P("narrow", "wide"),
            P(),
            P(),
        ),
        check_vma=False,
    )
```

```python
import math

import jax
import jax.numpy as jnp
from jax import lax
from jax.experimental import pallas as pl
from jax.experimental.pallas import tpu as pltpu
from jax.sharding import PartitionSpec as P

D = 1152
HEADS = 16
HEAD_DIM = 72
CAP = 4096
FREQ = 256
F = 16
S = 16
LCAP = 120


LEARNING_RATE = 0.04


def rounded(values):
    return values.astype(jnp.bfloat16)


def matmul(operand, matrix):
    return jnp.dot(operand, matrix, preferred_element_type=jnp.float32)


def matmul_tn(operand, matrix):
    return lax.dot_general(
        operand, matrix, (((0,), (0,)), ((), ())), preferred_element_type=jnp.float32
    )


def matmul_nt(operand, matrix):
    return lax.dot_general(
        operand, matrix, (((1,), (1,)), ((), ())), preferred_element_type=jnp.float32
    )


def sinusoid(places, feature):
    half_width = feature // 2
    freqs_row = jnp.exp(-math.log(10000.0) * jnp.arange(half_width, dtype=jnp.float32) / half_width)
    angles = places[:, None] * freqs_row[None, :]
    return jnp.concatenate([jnp.cos(angles), jnp.sin(angles)], axis=1)


def layer_norm(values):
    centred = values - jnp.mean(values, axis=-1, keepdims=True)
    return centred * lax.rsqrt(jnp.mean(centred * centred, axis=-1, keepdims=True) + 1e-06)


def modulate(values, shift_row, scale_row):
    return layer_norm(values) * (1.0 + scale_row) + shift_row


def head_window(head):
    first = HEAD_DIM * head
    low_lane = first // 128 * 128
    high_lane = -(-(first + HEAD_DIM) // 128) * 128
    return (first - low_lane, low_lane, high_lane)


def lanes_of_head(rows, head):
    offset, low_lane, high_lane = head_window(head)
    lane = lax.broadcasted_iota(jnp.int32, (rows, high_lane - low_lane), 1)
    return (lane >= offset) & (lane < offset + HEAD_DIM)


def dot_f32(left, right, contract):
    return lax.dot_general(
        left, right, ((contract[:1], contract[1:]), ((), ())), preferred_element_type=jnp.float32
    )


def softmax_rows(scores, allowed):
    scores = jnp.where(allowed, scores * HEAD_DIM ** (-0.5), -1000000000.0)
    powers = jnp.exp(scores - jnp.max(scores, axis=-1, keepdims=True))
    return powers * (1.0 / jnp.sum(powers, axis=-1, keepdims=True))


class HeadSums:
    def __init__(self, ref, base):
        self.ref = ref
        self.base = base
        self.tiles = {}

    def add(self, head, values):
        _, low_lane, high_lane = head_window(head)
        for tile in range(low_lane // 128, high_lane // 128):
            start = 128 * tile - low_lane
            share = values[:, start : start + 128]
            self.tiles[tile] = self.tiles[tile] + share if tile in self.tiles else share
        done = D // 128 if head == HEADS - 1 else HEAD_DIM * (head + 1) // 128
        for tile in [at for at in self.tiles if at < done]:
            start = self.base + 128 * tile
            self.ref[:, start : start + 128] = self.tiles.pop(tile).astype(self.ref.dtype)


def head_lanes(ref, base, head):
    _, low_lane, high_lane = head_window(head)
    values = ref[:, base + low_lane : base + high_lane]
    return jnp.where(lanes_of_head(values.shape[0], head), values, jnp.zeros_like(values))


def attend_heads(query_ref, key_ref, key_base, value_ref, value_base, out_ref, allowed):
    sums = HeadSums(out_ref, 0)
    for head in range(HEADS):
        _, low_lane, high_lane = head_window(head)
        query = head_lanes(query_ref, 0, head)
        key = key_ref[:, key_base + low_lane : key_base + high_lane]
        weights = softmax_rows(dot_f32(query, key, (1, 1)), allowed)
        value = head_lanes(value_ref, value_base, head)
        sums.add(head, dot_f32(rounded(weights), value, (1, 0)))


def attend_heads_back(
    query_ref, key_ref, key_base, value_ref, value_base, grad_ref,
    grad_query_ref, grad_key_ref, grad_value_ref, allowed,
):
    query_sums = HeadSums(grad_query_ref, 0)
    key_sums = HeadSums(grad_key_ref, key_base)
    value_sums = HeadSums(grad_value_ref, value_base)
    for head in range(HEADS):
        _, low_lane, high_lane = head_window(head)
        query = head_lanes(query_ref, 0, head)
        key = head_lanes(key_ref, key_base, head)
        value = value_ref[:, value_base + low_lane : value_base + high_lane]
        grad = head_lanes(grad_ref, 0, head)
        weights = softmax_rows(dot_f32(query, key, (1, 1)), allowed)
        grad_weights = dot_f32(grad, value, (1, 1))
        value_sums.add(head, dot_f32(rounded(weights), grad, (0, 0)))
        grad_scores = weights * (
            grad_weights - jnp.sum(grad_weights * weights, axis=-1, keepdims=True)
        )
        grad_low = rounded(grad_scores * HEAD_DIM ** (-0.5))
        query_sums.add(head, dot_f32(grad_low, key, (1, 0)))
        key_sums.add(head, dot_f32(grad_low, query, (0, 0)))


def same_group(rows, spatial):
    row = lax.broadcasted_iota(jnp.int32, (rows, rows), 0)
    column = lax.broadcasted_iota(jnp.int32, (rows, rows), 1)
    if spatial:
        return row // S == column // S
    return row % S == column % S


VMEM_LIMIT = pltpu.CompilerParams(vmem_limit_bytes=48 * 1024 * 1024)


def self_attend(qkv, spatial):
    rows = F * S

    def kernel(qkv_ref, out_ref):
        attend_heads(qkv_ref, qkv_ref, D, qkv_ref, 2 * D, out_ref, same_group(rows, spatial))

    return pl.pallas_call(
        kernel,
        grid=(qkv.shape[0] // rows,),
        in_specs=[pl.BlockSpec((rows, 3 * D), lambda i: (i, 0))],
        out_specs=pl.BlockSpec((rows, D), lambda i: (i, 0)),
        out_shape=jax.ShapeDtypeStruct((qkv.shape[0], D), jnp.bfloat16),
        compiler_params=VMEM_LIMIT,
        name="self_attend",
    )(qkv)


def self_attend_back(qkv, grad_mix, spatial):
    rows = F * S

    def kernel(qkv_ref, grad_ref, out_ref):
        attend_heads_back(
            qkv_ref, qkv_ref, D, qkv_ref, 2 * D, grad_ref,
            out_ref, out_ref, out_ref, same_group(rows, spatial),
        )

    return pl.pallas_call(
        kernel,
        grid=(qkv.shape[0] // rows,),
        in_specs=[
            pl.BlockSpec((rows, 3 * D), lambda i: (i, 0)),
            pl.BlockSpec((rows, D), lambda i: (i, 0)),
        ],
        out_specs=pl.BlockSpec((rows, 3 * D), lambda i: (i, 0)),
        out_shape=jax.ShapeDtypeStruct(qkv.shape, jnp.bfloat16),
        compiler_params=VMEM_LIMIT,
        name="self_attend_back",
    )(qkv, grad_mix)


def caption_mask(length):
    return lax.broadcasted_iota(jnp.int32, (F * S, LCAP), 1) < length


def cross_attend(query, pairs, lengths):
    clips = pairs.shape[0]

    def kernel(length_ref, query_ref, pair_ref, out_ref):
        allowed = caption_mask(length_ref[pl.program_id(0)])
        attend_heads(query_ref, pair_ref.at[0], 0, pair_ref.at[0], D, out_ref, allowed)

    return pl.pallas_call(
        kernel,
        grid_spec=pltpu.PrefetchScalarGridSpec(
            num_scalar_prefetch=1,
            grid=(clips,),
            in_specs=[
                pl.BlockSpec((F * S, D), lambda i, lens: (i, 0)),
                pl.BlockSpec((1, LCAP, 2 * D), lambda i, lens: (i, 0, 0)),
            ],
            out_specs=pl.BlockSpec((F * S, D), lambda i, lens: (i, 0)),
        ),
        out_shape=jax.ShapeDtypeStruct(query.shape, jnp.bfloat16),
        compiler_params=VMEM_LIMIT,
        name="cross_attend",
    )(lengths, query, pairs)


def cross_attend_back(query, pairs, grad_mix, lengths):
    clips = pairs.shape[0]

    def kernel(length_ref, query_ref, pair_ref, grad_ref, grad_query_ref, grad_pair_ref):
        allowed = caption_mask(length_ref[pl.program_id(0)])
        attend_heads_back(
            query_ref, pair_ref.at[0], 0, pair_ref.at[0], D, grad_ref,
            grad_query_ref, grad_pair_ref.at[0], grad_pair_ref.at[0], allowed,
        )

    return pl.pallas_call(
        kernel,
        grid_spec=pltpu.PrefetchScalarGridSpec(
            num_scalar_prefetch=1,
            grid=(clips,),
            in_specs=[
                pl.BlockSpec((F * S, D), lambda i, lens: (i, 0)),
                pl.BlockSpec((1, LCAP, 2 * D), lambda i, lens: (i, 0, 0)),
                pl.BlockSpec((F * S, D), lambda i, lens: (i, 0)),
            ],
            out_specs=[
                pl.BlockSpec((F * S, D), lambda i, lens: (i, 0)),
                pl.BlockSpec((1, LCAP, 2 * D), lambda i, lens: (i, 0, 0)),
            ],
        ),
        out_shape=[
            jax.ShapeDtypeStruct(query.shape, jnp.bfloat16),
            jax.ShapeDtypeStruct(pairs.shape, jnp.bfloat16),
        ],
        compiler_params=VMEM_LIMIT,
        name="cross_attend_back",
    )(lengths, query, pairs, grad_mix)


class Place:
    def __init__(self):
        self.wide = lax.axis_size("wide")
        self.narrow = lax.axis_size("narrow")
        self.depth = self.wide // 4
        self.half = self.depth // 2
        self.at = lax.axis_index("wide")
        self.core = self.at & 1
        self.x = (self.at >> 1) & 1
        self.z = self.at >> 2
        self.y = lax.axis_index("narrow")

    def over_wide(self, values, bit):
        return lax.ppermute(values, "wide", [(i, i ^ bit) for i in range(self.wide)])

    def over_core(self, values):
        return self.over_wide(values, 1)

    def over_x(self, values):
        return self.over_wide(values, 2)

    def over_z(self, values, bit):
        return self.over_wide(values, 4 * bit)

    def to_owner(self, values):
        pairs = [
            (i, i ^ 4 * self.half)
            for i in range(self.wide)
            if (i >> 2) // self.half != i & 1
        ]
        return lax.ppermute(values, "wide", pairs)

    def from_owner(self, values):
        pairs = [(i, i ^ 1) for i in range(self.wide) if (i >> 2) // self.half == i & 1]
        return lax.ppermute(values, "wide", pairs)

    def over_y(self, values, bit):
        return lax.ppermute(values, "narrow", [(i, i ^ bit) for i in range(self.narrow)])


def pair_up(bit, own, other):
    first = bit == 0
    return jnp.where(first, own, other), jnp.where(first, other, own)


def bits_of(size):
    return [1 << at for at in range(size.bit_length() - 1)]


def hold(values, others):
    if not others:
        return values
    kept, _ = lax.optimization_barrier((values, others))
    return kept


class Ticks:
    def __init__(self, joint):
        self.joint = joint
        self.ended = {True: [], False: []}
        self.sent = []

    def run(self, jobs, others=()):
        self.before = self.ended[True]
        ended = {True: [], False: []}
        before = dict(self.ended)
        if self.joint:
            before = {kind: list(before.values()) for kind in before}
            self.ended = {True: [], False: []}
        self.sent = []
        results = []
        for kind in (True, False):
            mine = [job for job in jobs if job.planar == kind]
            if not mine:
                continue
            values = [[value for value, _ in job.sends] for job in mine]
            values = hold(values, [before[kind], list(others)])
            self.sent.append(values)
            for job, held in zip(mine, values):
                result = [exchange(value) for value, (_, exchange) in zip(held, job.sends)]
                ended[kind].append(result)
                results.append((job, result))
            self.ended[kind] = ended[kind]
        for job, result in results:
            job.take(result)

    def during(self, values):
        return hold(values, [self.sent, self.before])

    def after(self, values):
        return hold(values, self.ended[True])


class Job:
    planar = False

    def __init__(self, transfers):
        self.transfers = transfers
        self.sends = next(transfers)

    def take(self, results):
        try:
            self.sends = self.transfers.send(results)
        except StopIteration:
            self.sends = None


def spread_y(place, values):
    pieces = [values]
    for bit in bits_of(place.narrow):
        pieces = pieces + [place.over_y(piece, bit) for piece in pieces]
    return pieces[1:]


class Gather(Job):
    def __init__(self, place, own):
        self.place = place
        super().__init__(self.plan(own[None]))

    def plan(self, block):
        place = self.place
        half = place.half
        for bit in bits_of(half):
            [other] = yield [(block, lambda values, bit=bit: place.over_z(values, bit))]
            block = jnp.concatenate(pair_up(place.z & bit, block, other))
        quarter = half // 2
        low, high = block[:quarter], block[quarter:]
        [low_away] = yield [(low, lambda values: place.over_z(values, half))]
        [high_away] = yield [(high, lambda values: place.over_z(values, half))]
        low = pair_up(place.z & half, low, low_away)
        high = pair_up(place.z & half, high, high_away)
        block = jnp.concatenate([low[0], high[0], low[1], high[1]])
        self.planar = True
        by_x, by_y = yield [(block, place.over_x), (block, lambda values: spread_y(place, values))]
        far_xy, near_xy = yield [
            (jnp.stack([piece[half:] for piece in by_y]), place.over_x),
            (by_x[:half], lambda values: spread_y(place, values)),
        ]
        columns = block.shape[-1] * place.narrow
        mine = unwritten((place.depth, 2, block.shape[1], columns))
        parts = (
            (0, 0, self.lanes([block] + list(by_y))),
            (0, 1, self.lanes([by_x[:half]] + list(near_xy))),
            (half, 1, self.lanes([by_x[half:]] + [far_xy[at] for at in range(place.narrow - 1)])),
        )
        for first_z, apart, part in parts:
            mine = lax.dynamic_update_slice(
                mine, part[:, None], (first_z, place.x ^ apart, 0, 0)
            )
        self.mine = mine
        self.planar = False
        [self.other] = yield [(mine, place.over_core)]

    def lanes(self, pieces):
        place = self.place
        if place.narrow == 1:
            return pieces[0]
        if place.narrow == 2:
            return jnp.concatenate(pair_up(place.y, pieces[0], pieces[1]), axis=-1)
        return jnp.concatenate(
            [lax.select_n(place.y ^ spot, *pieces) for spot in range(place.narrow)], axis=-1
        )

    def whole(self, first_row, rows):
        place = self.place
        span = slice(first_row, first_row + rows)
        columns = self.mine.shape[-1]
        whole = unwritten((place.depth, 2, 2, rows, columns))
        for part, core in ((self.mine, place.core), (self.other, 1 - place.core)):
            whole = lax.dynamic_update_slice(
                whole, part[:, :, None, span], (0, 0, core, 0, 0)
            )
        return whole.reshape(place.wide * rows, columns)


def unwritten(shape):
    return pl.pallas_call(
        lambda out_ref: None,
        out_specs=pl.BlockSpec(memory_space=pl.ANY),
        out_shape=jax.ShapeDtypeStruct(shape, jnp.bfloat16),
        name="unwritten",
    )()


def side(values, bit, axis):
    return lax.dynamic_index_in_dim(values, bit, axis, keepdims=False)


def columns_at(values, index, count):
    width = values.shape[-1] // count
    if count == 1:
        return values
    if count == 2:
        return jnp.where(index == 0, values[..., :width], values[..., width:])
    return lax.dynamic_slice_in_dim(values, index * width, width, axis=values.ndim - 1)


def wide_float(values):
    return values.astype(jnp.float32)


def reduce_y(place, values):
    for bit in reversed(bits_of(place.narrow)):
        upper = ((place.y & bit) != 0).astype(jnp.int32)
        away = place.over_y(rounded(columns_at(values, 1 - upper, 2)), bit)
        values = columns_at(values, upper, 2) + wide_float(away)
    return values


class Scatter(Job):
    def __init__(self, place, products):
        self.place = place
        super().__init__(self.plan(products))

    def plan(self, products):
        place = self.place
        spread = place.half
        quarter = spread // 2
        sends = [(grad, place.over_core) for _, _, grad, *known in products if len(known) == 1]
        away = iter((yield sends) if sends else ())
        views = []
        for operand, operand_away, grad, parts, *known in products:
            grad_away = known[0] if known else next(away)
            kept = matmul_tn(columns_at(operand, place.core, 2), grad)
            total = matmul_tn(columns_at(operand_away, place.core, 2), grad_away)
            total = rounded(total + wide_float(rounded(kept)))
            width = grad.shape[1] // parts
            for part in range(parts):
                view = total[:, part * width : (part + 1) * width]
                views.append(view.reshape(spread, 2, -1, width))

        def summed(span, x_bit=None):
            mine = [view[span] for view in views]
            if x_bit is not None:
                mine = [side(view, x_bit, 1) for view in mine]
            return jnp.concatenate(mine, axis=-2) if len(mine) > 1 else mine[0]

        near_span, far_span = slice(0, quarter), slice(quarter, None)
        self.planar = True
        if place.narrow == 2:
            near_away, far_away = yield [
                (summed(near_span, 1 - place.x), place.over_x),
                (
                    columns_at(summed(far_span), 1 - place.y, 2),
                    lambda values: place.over_y(values, 1),
                ),
            ]

            def near(y_bit):
                mine = columns_at(summed(near_span, place.x), y_bit, 2)
                return wide_float(mine) + wide_float(columns_at(near_away, y_bit, 2))

            def far(x_bit):
                mine = columns_at(summed(far_span, x_bit), place.y, 2)
                return wide_float(mine) + wide_float(side(far_away, x_bit, 1))

            near_back, far_back = yield [
                (rounded(near(1 - place.y)), lambda values: place.over_y(values, 1)),
                (rounded(far(1 - place.x)), place.over_x),
            ]
            near = near(place.y) + wide_float(near_back)
            far = far(place.x) + wide_float(far_back)
        else:
            near_away, far = yield [
                (summed(near_span, 1 - place.x), place.over_x),
                (wide_float(summed(far_span)), lambda values: reduce_y(place, values)),
            ]
            near = wide_float(summed(near_span, place.x)) + wide_float(near_away)
            near, far_back = yield [
                (near, lambda values: reduce_y(place, values)),
                (rounded(side(far, 1 - place.x, 1)), place.over_x),
            ]
            far = side(far, place.x, 1) + wide_float(far_back)
        self.planar = False
        total, sent = pair_up(place.z & quarter, near, far)
        [away] = yield [(rounded(sent), lambda values: place.over_z(values, quarter))]
        total = total + wide_float(away)
        for bit in reversed(bits_of(quarter)):
            total = total.reshape((2, total.shape[0] // 2) + total.shape[1:])
            upper = ((place.z & bit) != 0).astype(jnp.int32)
            [away] = yield [
                (
                    rounded(side(total, 1 - upper, 0)),
                    lambda values, bit=bit: place.over_z(values, bit),
                )
            ]
            total = side(total, upper, 0) + wide_float(away)
        total = total[0]
        [away] = yield [(rounded(total), place.to_owner)]
        total = total + wide_float(away)
        pieces, first = [], 0
        for view in views:
            rows = view.shape[2]
            pieces.append(total[first : first + rows].reshape(2, rows // 2, -1))
            first += rows
        sent = [side(piece, 1 - place.core, 0) for piece in pieces]
        sent = jnp.concatenate(sent) if len(sent) > 1 else sent[0]
        [away] = yield [(sent, place.from_owner)]
        owner = place.z // spread == place.core
        self.total, first = [], 0
        for piece in pieces:
            rows = piece.shape[1]
            theirs = away[first : first + rows]
            self.total.append(jnp.where(owner, side(piece, place.core, 0), theirs))
            first += rows


class Reducer:
    def __init__(self, place):
        self.place = place
        self.ticks = Ticks(False)
        self.jobs = []

    def add(self, *products):
        job = Scatter(self.place, products)
        self.jobs.append(job)
        return job

    def run(self, *others, wait=()):
        due = [job for job in self.jobs if job.sends is not None and job not in wait]
        if due:
            self.ticks.run(due, others)
        return bool(due)


def adam_update(master, first_moment, second_moment, gradient, step_value):
    first_new = 0.9 * first_moment + 0.1 * gradient
    second_new = 0.999 * second_moment + 0.001 * gradient * gradient
    first_hat = first_new / (1.0 - 0.9**step_value)
    second_hat = second_new / (1.0 - 0.999**step_value)
    master_new = master - LEARNING_RATE * (
        first_hat / (jnp.sqrt(second_hat) + 1e-08) + 0.01 * master
    )
    return (master_new, first_new, second_new)


def body(
    projections,
    qkv_weights,
    mlp_weights,
    ada_weights,
    entry_weights,
    patch_weights,
    shift_tables,
    first_projections,
    first_qkv_weights,
    first_mlp_weights,
    first_ada_weights,
    first_entry_weights,
    first_patch_weights,
    first_shift_tables,
    second_projections,
    second_qkv_weights,
    second_mlp_weights,
    second_ada_weights,
    second_entry_weights,
    second_patch_weights,
    second_shift_tables,
    latents,
    noise,
    captions,
    cap_len,
    timesteps,
    step_count,
):
    shards = (
        projections,
        qkv_weights,
        mlp_weights,
        ada_weights,
        entry_weights,
        patch_weights,
        shift_tables,
    )
    firsts = (
        first_projections,
        first_qkv_weights,
        first_mlp_weights,
        first_ada_weights,
        first_entry_weights,
        first_patch_weights,
        first_shift_tables,
    )
    seconds = (
        second_projections,
        second_qkv_weights,
        second_mlp_weights,
        second_ada_weights,
        second_entry_weights,
        second_patch_weights,
        second_shift_tables,
    )
    place = Place()
    clips = latents.shape[0]
    tokens = F * S
    video_count = clips * place.wide * place.narrow
    rows = projections.shape[1]
    entry_rows = entry_weights.shape[0]

    def by_clip(values):
        return values.reshape(clips, tokens, values.shape[-1])

    def flat(values):
        return values.reshape(clips * tokens, values.shape[-1])

    devices = place.wide * place.narrow
    all_clips = clips * devices

    def to_all(values):
        return lax.all_to_all(values, ("wide", "narrow"), split_axis=0, concat_axis=0, tiled=True)

    def columns_to_all(values):
        pieces = values.reshape(values.shape[0], place.narrow, -1).transpose(1, 0, 2)
        pieces = jnp.broadcast_to(pieces[None], (place.wide,) + pieces.shape)
        return to_all(pieces.reshape((devices,) + pieces.shape[2:]))

    proj_low, qkv_low, mlp_low, ada_low, entry_low, patch_low, table_low = (
        rounded(shard) for shard in shards
    )
    width = projections.shape[2]
    small = jnp.concatenate([patch_low.reshape(-1), table_low.reshape(-1)])
    small_rows = -(-small.shape[0] // (8 * width)) * 8
    small = jnp.pad(small, (0, small_rows * width - small.shape[0])).reshape(small_rows, width)
    ticks = Ticks(True)
    gathers = [
        Gather(place, own)
        for own in (
            jnp.concatenate([proj_low[:2].reshape(2 * rows, width), small]),
            entry_low,
            qkv_low.reshape(2 * rows, -1),
            proj_low[2:].reshape(6 * rows, width),
            mlp_low[0],
            mlp_low[1],
        )
    ]
    early, entry_gather, qkv_gather, late, mlp_in_gather, mlp_out_gather = gathers
    rounds = iter(range(2 * len(gathers) + len(bits_of(place.depth)) + 4))

    def gather_on(*others):
        now = next(rounds)
        due = [job for at, job in enumerate(gathers) if job.sends is not None and now >= 2 * at]
        if due:
            ticks.run(due, others)

    while early.sends is not None:
        gather_on()
    small_all = early.whole(2 * rows, small_rows)
    proj_all = [early.whole(0, rows), early.whole(rows, rows)]
    small_all = small_all.reshape(place.wide, small_rows, place.narrow, width).transpose(0, 2, 1, 3)
    small_all = small_all.reshape(place.wide, place.narrow, small_rows * width)
    patch_count = patch_low.size
    patch_all = small_all[:, :, :patch_count].reshape(
        (place.wide, place.narrow) + patch_low.shape
    )
    patch_all = patch_all.transpose(2, 0, 3, 1, 4).reshape(2, D, -1)
    table_all = small_all[:, :, patch_count : patch_count + table_low.size].reshape(
        (place.wide, place.narrow) + table_low.shape
    )
    table_all = table_all.transpose(1, 2, 0, 3).reshape(8, D).astype(jnp.float32)

    time_value = timesteps.astype(jnp.float32)
    signal = jnp.cos((time_value / 1000.0 + 0.008) / 1.008 * (math.pi / 2)) ** 2
    noise_rows = flat(noise.astype(jnp.float32))
    noised_low = rounded(
        flat(
            jnp.sqrt(signal)[:, None, None] * latents.astype(jnp.float32)
            + jnp.sqrt(1.0 - signal)[:, None, None] * noise.astype(jnp.float32)
        )
    )
    spatial_pos = jnp.tile(sinusoid(jnp.arange(S, dtype=jnp.float32), D), (clips * F, 1))
    frame_pos = jnp.tile(jnp.repeat(sinusoid(jnp.arange(F, dtype=jnp.float32), D), S, 0), (clips, 1))
    embed_low = rounded(sinusoid(time_value, FREQ))
    while entry_gather.sends is not None:
        gather_on(patch_all, table_all)
    gather_on()
    entry_gather.other = ticks.during(entry_gather.other)
    entry_all = entry_gather.whole(0, entry_rows)
    time_inner = matmul(embed_low, entry_all[CAP:])
    inner_low = rounded(jax.nn.silu(time_inner))
    time_embed = matmul(inner_low, proj_all[0])
    embed_act = rounded(jax.nn.silu(time_embed))

    def by_rows(values):
        return values.reshape(clips, place.wide, rows).transpose(1, 0, 2)

    sent = jnp.concatenate(
        [
            by_rows(embed_act),
            by_rows(inner_low),
            jnp.broadcast_to(embed_low[None], (place.wide,) + embed_low.shape),
        ],
        axis=-1,
    )
    sent = jnp.broadcast_to(sent[:, None], (place.wide, place.narrow) + sent.shape[1:])
    gather_on(sent, entry_all)
    sent = ticks.during(sent)
    sent = to_all(sent.reshape((devices,) + sent.shape[2:])).reshape(all_clips, -1)
    my_embed_act, my_inner, embed_all = sent[:, :rows], sent[:, rows : 2 * rows], sent[:, 2 * rows :]
    part = matmul(my_embed_act, ada_low).reshape(devices, clips, -1)

    caption_rows = captions.reshape(clips * LCAP, CAP)
    caption_wide = jnp.pad(caption_rows, ((0, 0), (0, place.wide * entry_rows - CAP)))
    caption_inner = matmul(ticks.during(caption_rows), entry_all[:CAP])
    caption_act = rounded(jax.nn.gelu(caption_inner))
    context_low = rounded(matmul(caption_act, proj_all[1]))
    gather_on(context_low, part)
    part = to_all(ticks.during(part))
    qkv_gather.other = ticks.during(qkv_gather.other)
    qkv_all = [qkv_gather.whole(0, rows), qkv_gather.whole(rows, rows)]
    part = part.reshape(place.wide, place.narrow, clips, -1)
    modulations = jnp.sum(part, axis=0).transpose(1, 0, 2).reshape(clips, 6, D) + table_all[:6]
    caption_wide_away = place.over_core(caption_wide)
    caption_act_away = place.over_core(caption_act)
    context_low_away = place.over_core(context_low)
    gather_on(modulations, caption_wide_away, caption_act_away, context_low_away, *qkv_all)
    modulations = ticks.during(modulations)
    shift_a, scale_a, gate_a, shift_m, scale_m, gate_m = (
        modulations[:, at : at + 1] for at in range(6)
    )
    final_shift = (time_embed + table_all[6])[:, None]
    final_scale = (time_embed + table_all[7])[:, None]

    hidden = matmul_nt(noised_low, patch_all[0]) + spatial_pos
    normed_spatial = rounded(flat(modulate(by_clip(hidden), shift_a, scale_a)))
    spatial_qkv = rounded(matmul(normed_spatial, qkv_all[0]))
    normed_spatial_away = place.over_core(normed_spatial)
    gather_on(spatial_qkv, normed_spatial_away)
    late.other = ticks.during(late.other)
    proj_all = proj_all + [late.whole(at * rows, rows) for at in range(6)]
    pair_weight = jnp.concatenate([proj_all[5], proj_all[6]], axis=1)
    spatial_mix = self_attend(ticks.during(spatial_qkv), True)
    gather_on(spatial_mix, pair_weight, *proj_all)
    spatial_mix, context_low = ticks.during((spatial_mix, context_low))
    cross_pairs = rounded(matmul(context_low, pair_weight))
    spatial_out = matmul(spatial_mix, proj_all[2])
    hidden_one = hidden + flat(gate_a * by_clip(spatial_out))
    temporal_in = rounded(hidden_one + frame_pos)
    temporal_qkv = rounded(matmul(temporal_in, qkv_all[1]))
    spatial_mix_away = place.over_core(spatial_mix)
    temporal_in_away = place.over_core(temporal_in)
    gather_on(cross_pairs, temporal_qkv, spatial_mix_away, temporal_in_away)
    temporal_mix = self_attend(ticks.during(temporal_qkv), False)
    mlp_in_gather.other = ticks.during(mlp_in_gather.other)
    mlp_in = mlp_in_gather.whole(0, rows)
    temporal_out = matmul(temporal_mix, proj_all[3])
    hidden_two = hidden_one + flat(gate_a * by_clip(temporal_out))
    hidden_two_low = rounded(hidden_two)
    temporal_mix_away = place.over_core(temporal_mix)
    hidden_two_low_away = place.over_core(hidden_two_low)
    cross_query = rounded(matmul(hidden_two_low, proj_all[4]))
    while mlp_out_gather.sends is not None:
        gather_on(cross_query, mlp_in)
    mlp_out = mlp_out_gather.whole(0, rows)
    cross_mix = cross_attend(cross_query, cross_pairs.reshape(clips, LCAP, 2 * D), cap_len)
    cross_mix_away = place.over_core(cross_mix)
    hidden_three = hidden_two + matmul(cross_mix, proj_all[7])
    normed_mlp = rounded(flat(modulate(by_clip(hidden_three), shift_m, scale_m)))
    normed_mlp_away = place.over_core(normed_mlp)
    expand = matmul(normed_mlp, mlp_in)
    expand_act = rounded(jax.nn.gelu(expand))
    expand_act_away = place.over_core(expand_act)
    contract = matmul_nt(expand_act, mlp_out)
    hidden_four = hidden_three + flat(gate_m * by_clip(contract))
    final_low = rounded(flat(modulate(by_clip(hidden_four), final_shift, final_scale)))
    misfit = matmul(final_low, patch_all[1]) - noise_rows
    entries = tokens * latents.shape[2]
    loss_value = jnp.sum(misfit * misfit) / (entries * video_count)

    grad_pred = rounded(2.0 * misfit / (entries * video_count))
    grad_patch_out = matmul_tn(final_low, grad_pred)
    _, pull_final = jax.vjp(modulate, by_clip(hidden_four), final_shift, final_scale)
    grad_four, grad_fshift, grad_fscale = pull_final(by_clip(matmul_nt(grad_pred, patch_all[1])))
    grad_contract = rounded(flat(grad_four * gate_m))
    grad_gate_mlp = jnp.sum(grad_four * by_clip(contract), axis=1)
    reducer = Reducer(place)
    during, after = reducer.ticks.during, reducer.ticks.after
    grad_contract_away = place.over_core(grad_contract)
    mlp_out_scatter = reducer.add(
        (grad_contract, grad_contract_away, expand_act, 1, expand_act_away)
    )
    reducer.run()
    _, pull_gelu = jax.vjp(jax.nn.gelu, expand)
    grad_expand = rounded(pull_gelu(matmul(during(grad_contract), mlp_out))[0])
    mlp_in_scatter = reducer.add((normed_mlp, normed_mlp_away, grad_expand, 1))
    reducer.run()
    _, pull_mlp_norm = jax.vjp(modulate, by_clip(hidden_three), shift_m, scale_m)
    grad_three_part, grad_shift_mlp, grad_scale_mlp = pull_mlp_norm(
        by_clip(matmul_nt(during(grad_expand), mlp_in))
    )
    grad_three = flat(grad_four + grad_three_part)
    grad_cross_out = rounded(grad_three)
    reducer.run(grad_cross_out)
    grad_cross_mix = rounded(matmul_nt(during(grad_cross_out), proj_all[7]))
    grad_query_low, grad_pairs_low = cross_attend_back(
        cross_query, cross_pairs.reshape(clips, LCAP, 2 * D), grad_cross_mix, cap_len
    )
    grad_pairs_low = grad_pairs_low.reshape(clips * LCAP, 2 * D)
    grad_context = rounded(matmul_nt(grad_pairs_low, pair_weight))
    caption_scatter = reducer.add(
        (caption_act, caption_act_away, grad_context, 1),
        (context_low, context_low_away, grad_pairs_low, 2),
    )
    reducer.run(grad_query_low)
    _, pull_caption = jax.vjp(jax.nn.gelu, caption_inner)
    grad_context, grad_query_low = during((grad_context, grad_query_low))
    grad_caption_inner = rounded(pull_caption(matmul_nt(grad_context, proj_all[1]))[0])
    grad_two = grad_three + matmul_nt(grad_query_low, proj_all[4])
    grad_temporal_out = rounded(flat(by_clip(grad_two) * gate_a))
    grad_gate_attn = jnp.sum(by_clip(grad_two * temporal_out), axis=1)
    grad_temporal_mix = rounded(matmul_nt(grad_temporal_out, proj_all[3]))
    reducer.run(grad_temporal_mix, grad_caption_inner)
    grad_temporal_qkv = self_attend_back(temporal_qkv, during(grad_temporal_mix), False)
    entry_scatter = reducer.add((caption_wide, caption_wide_away, grad_caption_inner, 1))
    qkv_one_scatter = reducer.add((temporal_in, temporal_in_away, grad_temporal_qkv, 1))
    reducer.run()
    grad_one = grad_two + matmul_nt(during(grad_temporal_qkv), qkv_all[1])
    grad_spatial_out = rounded(flat(by_clip(grad_one) * gate_a))
    grad_gate_attn = grad_gate_attn + jnp.sum(by_clip(grad_one * spatial_out), axis=1)
    grad_spatial_mix = rounded(matmul_nt(grad_spatial_out, proj_all[2]))
    reducer.run(grad_spatial_mix, wait=(qkv_one_scatter,))
    grad_spatial_qkv = self_attend_back(spatial_qkv, during(grad_spatial_mix), True)
    qkv_zero_scatter = reducer.add((normed_spatial, normed_spatial_away, grad_spatial_qkv, 1))
    reducer.run(wait=(qkv_one_scatter,))
    grad_normed_spatial = matmul_nt(during(grad_spatial_qkv), qkv_all[0])
    square_scatter = reducer.add(
        (spatial_mix, spatial_mix_away, grad_spatial_out, 1),
        (temporal_mix, temporal_mix_away, grad_temporal_out, 1),
        (hidden_two_low, hidden_two_low_away, grad_query_low, 1),
        (cross_mix, cross_mix_away, grad_cross_out, 1),
    )
    reducer.run(grad_normed_spatial, wait=(qkv_zero_scatter,))
    grad_normed_spatial = during(grad_normed_spatial)
    reducer.run(wait=(qkv_zero_scatter, square_scatter))
    reducer.run(wait=(square_scatter,))
    qkv_zero_started = reducer.ticks.sent
    reducer.run(wait=(square_scatter,))
    reducer.run()
    middle = reducer.ticks.sent
    while reducer.run():
        pass
    sum_mlp_in, sum_mlp_out = mlp_in_scatter.total[0], mlp_out_scatter.total[0]
    sum_qkv_one = qkv_one_scatter.total[0]
    sum_qkv_zero = qkv_zero_scatter.total[0]
    sum_two, sum_three, sum_four, sum_seven = square_scatter.total
    sum_one, sum_five, sum_six = caption_scatter.total
    sum_entry = entry_scatter.total[0]
    _, pull_spatial_norm = jax.vjp(modulate, by_clip(hidden), shift_a, scale_a)
    grad_hidden_part, grad_shift_attn, grad_scale_attn = pull_spatial_norm(
        by_clip(grad_normed_spatial)
    )
    grad_hidden = rounded(grad_one + flat(grad_hidden_part))
    grad_patch_in = matmul_tn(grad_hidden, noised_low)
    grad_modulations = jnp.stack(
        [
            grad_shift_attn[:, 0],
            grad_scale_attn[:, 0],
            grad_gate_attn,
            grad_shift_mlp[:, 0],
            grad_scale_mlp[:, 0],
            grad_gate_mlp,
        ],
        axis=1,
    )

    grad_ada_out = hold(rounded(grad_modulations.reshape(clips, 6 * D)), qkv_zero_started)
    grad_ada_mine = columns_to_all(grad_ada_out).reshape(all_clips, -1)
    grad_ada = matmul_tn(my_embed_act, grad_ada_mine)
    grad_ada_mine = hold(grad_ada_mine, middle)
    act_part = to_all(matmul_nt(grad_ada_mine, ada_low).reshape(devices, clips, rows))
    act_part = jnp.sum(act_part.reshape(place.wide, place.narrow, clips, rows), axis=1)
    grad_embed_act = act_part.transpose(1, 0, 2).reshape(clips, D)
    _, pull_embed = jax.vjp(jax.nn.silu, time_embed)
    grad_time_embed = rounded(
        pull_embed(grad_embed_act)[0] + (grad_fshift + grad_fscale)[:, 0]
    )
    _, pull_inner = jax.vjp(jax.nn.silu, time_inner)
    grad_time_inner = rounded(pull_inner(matmul_nt(grad_time_embed, proj_all[0]))[0])
    time_rows = columns_to_all(jnp.concatenate([grad_time_embed, grad_time_inner]))
    grad_embed_mine = time_rows[:, :clips].reshape(all_clips, width)
    grad_inner_mine = time_rows[:, clips:].reshape(all_clips, width)
    grad_proj_zero = matmul_tn(my_inner, grad_embed_mine)
    grad_time_rows = matmul_tn(embed_all, grad_inner_mine)
    spot = jnp.clip((place.at + 1) * entry_rows - CAP, 0, FREQ + entry_rows)
    padded_rows = jnp.pad(grad_time_rows, ((entry_rows, entry_rows), (0, 0)))
    grad_entry_time = lax.dynamic_slice_in_dim(padded_rows, spot, entry_rows, axis=0)

    grad_tables = jnp.concatenate(
        [
            jnp.sum(grad_modulations, axis=0),
            jnp.sum(grad_fshift, axis=0),
            jnp.sum(grad_fscale, axis=0),
        ]
    )
    grad_patches = jnp.stack([grad_patch_in, grad_patch_out]).reshape(
        2, place.wide, rows, place.narrow, -1
    )
    grad_tables = grad_tables.reshape(place.narrow, -1, place.wide, rows)
    small_grads = jnp.concatenate(
        [
            grad_patches.transpose(1, 3, 0, 2, 4).reshape(devices, -1),
            grad_tables.transpose(2, 0, 1, 3).reshape(devices, -1),
        ],
        axis=1,
    )
    small_grads = jnp.sum(to_all(hold(small_grads, middle)), axis=0)
    sum_patch = small_grads[: patch_weights.size].reshape(patch_weights.shape)
    sum_tables = small_grads[patch_weights.size :].reshape(shift_tables.shape)

    sum_projections = jnp.stack(
        [
            grad_proj_zero,
            sum_one,
            sum_two,
            sum_three,
            sum_four,
            sum_five,
            sum_six,
            sum_seven,
        ]
    )
    summed = (
        sum_projections,
        jnp.stack([sum_qkv_zero, sum_qkv_one]),
        jnp.stack([sum_mlp_in, sum_mlp_out]),
        grad_ada,
        sum_entry + grad_entry_time,
        sum_patch,
        sum_tables,
    )
    square_part = sum((jnp.sum(piece * piece) for piece in summed))
    both = jnp.broadcast_to(jnp.stack([loss_value, square_part]), (devices, 2))
    loss_total, square_total = jnp.sum(to_all(both), axis=0)
    grad_norm = jnp.sqrt(square_total)
    threshold = (video_count * latents.shape[1]) ** (-0.5)
    factor = threshold / jnp.maximum(grad_norm, threshold)
    step_value = step_count[0].astype(jnp.float32)
    updated = [
        adam_update(master, first_moment, second_moment, gradient * factor, step_value)
        for master, first_moment, second_moment, gradient in zip(shards, firsts, seconds, summed)
    ]
    return (
        updated[0][0],
        updated[1][0],
        updated[2][0],
        updated[3][0],
        updated[4][0],
        updated[5][0],
        updated[6][0],
        updated[0][1],
        updated[1][1],
        updated[2][1],
        updated[3][1],
        updated[4][1],
        updated[5][1],
        updated[6][1],
        updated[0][2],
        updated[1][2],
        updated[2][2],
        updated[3][2],
        updated[4][2],
        updated[5][2],
        updated[6][2],
        loss_total,
        grad_norm,
    )


def solution(mesh):
    return jax.shard_map(
        body,
        mesh=mesh,
        in_specs=(
            P(None, "wide", "narrow"),
            P(None, "wide", "narrow"),
            P(None, "wide", "narrow"),
            P("wide", "narrow"),
            P("wide", "narrow"),
            P(None, "wide", "narrow"),
            P("narrow", "wide"),
            P(None, "wide", "narrow"),
            P(None, "wide", "narrow"),
            P(None, "wide", "narrow"),
            P("wide", "narrow"),
            P("wide", "narrow"),
            P(None, "wide", "narrow"),
            P("narrow", "wide"),
            P(None, "wide", "narrow"),
            P(None, "wide", "narrow"),
            P(None, "wide", "narrow"),
            P("wide", "narrow"),
            P("wide", "narrow"),
            P(None, "wide", "narrow"),
            P("narrow", "wide"),
            P(("wide", "narrow"), None, None),
            P(("wide", "narrow"), None, None),
            P(("wide", "narrow"), None, None),
            P(("wide", "narrow")),
            P(("wide", "narrow")),
            P(),
        ),
        out_specs=(
            P(None, "wide", "narrow"),
            P(None, "wide", "narrow"),
            P(None, "wide", "narrow"),
            P("wide", "narrow"),
            P("wide", "narrow"),
            P(None, "wide", "narrow"),
            P("narrow", "wide"),
            P(None, "wide", "narrow"),
            P(None, "wide", "narrow"),
            P(None, "wide", "narrow"),
            P("wide", "narrow"),
            P("wide", "narrow"),
            P(None, "wide", "narrow"),
            P("narrow", "wide"),
            P(None, "wide", "narrow"),
            P(None, "wide", "narrow"),
            P(None, "wide", "narrow"),
            P("wide", "narrow"),
            P("wide", "narrow"),
            P(None, "wide", "narrow"),
            P("narrow", "wide"),
            P(),
            P(),
        ),
        check_vma=False,
    )
```

```python
import math

import jax
import jax.numpy as jnp
from jax import lax
from jax.experimental import pallas as pl
from jax.experimental.pallas import tpu as pltpu
from jax.sharding import PartitionSpec as P

D = 1152
HEADS = 16
HEAD_DIM = 72
CAP = 4096
FREQ = 256
F = 16
S = 16
LCAP = 120


LEARNING_RATE = 0.04


def rounded(values):
    return values.astype(jnp.bfloat16)


def matmul(operand, matrix):
    return jnp.dot(operand, matrix, preferred_element_type=jnp.float32)


def matmul_tn(operand, matrix):
    return lax.dot_general(
        operand, matrix, (((0,), (0,)), ((), ())), preferred_element_type=jnp.float32
    )


def matmul_nt(operand, matrix):
    return lax.dot_general(
        operand, matrix, (((1,), (1,)), ((), ())), preferred_element_type=jnp.float32
    )


def sinusoid(places, feature):
    half_width = feature // 2
    freqs_row = jnp.exp(-math.log(10000.0) * jnp.arange(half_width, dtype=jnp.float32) / half_width)
    angles = places[:, None] * freqs_row[None, :]
    return jnp.concatenate([jnp.cos(angles), jnp.sin(angles)], axis=1)


def layer_norm(values):
    centred = values - jnp.mean(values, axis=-1, keepdims=True)
    return centred * lax.rsqrt(jnp.mean(centred * centred, axis=-1, keepdims=True) + 1e-06)


def modulate(values, shift_row, scale_row):
    return layer_norm(values) * (1.0 + scale_row) + shift_row


def head_window(head):
    first = HEAD_DIM * head
    low_lane = first // 128 * 128
    high_lane = -(-(first + HEAD_DIM) // 128) * 128
    return (first - low_lane, low_lane, high_lane)


def lanes_of_head(rows, head):
    offset, low_lane, high_lane = head_window(head)
    lane = lax.broadcasted_iota(jnp.int32, (rows, high_lane - low_lane), 1)
    return (lane >= offset) & (lane < offset + HEAD_DIM)


def dot_f32(left, right, contract):
    return lax.dot_general(
        left, right, ((contract[:1], contract[1:]), ((), ())), preferred_element_type=jnp.float32
    )


def softmax_rows(scores, allowed):
    scores = jnp.where(allowed, scores * HEAD_DIM ** (-0.5), -1000000000.0)
    powers = jnp.exp(scores - jnp.max(scores, axis=-1, keepdims=True))
    return powers * (1.0 / jnp.sum(powers, axis=-1, keepdims=True))


class HeadSums:
    def __init__(self, ref, base):
        self.ref = ref
        self.base = base
        self.tiles = {}

    def add(self, head, values):
        _, low_lane, high_lane = head_window(head)
        for tile in range(low_lane // 128, high_lane // 128):
            start = 128 * tile - low_lane
            share = values[:, start : start + 128]
            self.tiles[tile] = self.tiles[tile] + share if tile in self.tiles else share
        done = D // 128 if head == HEADS - 1 else HEAD_DIM * (head + 1) // 128
        for tile in [at for at in self.tiles if at < done]:
            start = self.base + 128 * tile
            self.ref[:, start : start + 128] = self.tiles.pop(tile).astype(self.ref.dtype)


def head_lanes(ref, base, head):
    _, low_lane, high_lane = head_window(head)
    values = ref[:, base + low_lane : base + high_lane]
    return jnp.where(lanes_of_head(values.shape[0], head), values, jnp.zeros_like(values))


def attend_heads(query_ref, key_ref, key_base, value_ref, value_base, out_ref, allowed):
    sums = HeadSums(out_ref, 0)
    for head in range(HEADS):
        _, low_lane, high_lane = head_window(head)
        query = head_lanes(query_ref, 0, head)
        key = key_ref[:, key_base + low_lane : key_base + high_lane]
        weights = softmax_rows(dot_f32(query, key, (1, 1)), allowed)
        value = head_lanes(value_ref, value_base, head)
        sums.add(head, dot_f32(rounded(weights), value, (1, 0)))


def attend_heads_back(
    query_ref, key_ref, key_base, value_ref, value_base, grad_ref,
    grad_query_ref, grad_key_ref, grad_value_ref, allowed,
):
    query_sums = HeadSums(grad_query_ref, 0)
    key_sums = HeadSums(grad_key_ref, key_base)
    value_sums = HeadSums(grad_value_ref, value_base)
    for head in range(HEADS):
        _, low_lane, high_lane = head_window(head)
        query = head_lanes(query_ref, 0, head)
        key = head_lanes(key_ref, key_base, head)
        value = value_ref[:, value_base + low_lane : value_base + high_lane]
        grad = head_lanes(grad_ref, 0, head)
        weights = softmax_rows(dot_f32(query, key, (1, 1)), allowed)
        grad_weights = dot_f32(grad, value, (1, 1))
        value_sums.add(head, dot_f32(rounded(weights), grad, (0, 0)))
        grad_scores = weights * (
            grad_weights - jnp.sum(grad_weights * weights, axis=-1, keepdims=True)
        )
        grad_low = rounded(grad_scores * HEAD_DIM ** (-0.5))
        query_sums.add(head, dot_f32(grad_low, key, (1, 0)))
        key_sums.add(head, dot_f32(grad_low, query, (0, 0)))


def same_group(rows, spatial):
    row = lax.broadcasted_iota(jnp.int32, (rows, rows), 0)
    column = lax.broadcasted_iota(jnp.int32, (rows, rows), 1)
    if spatial:
        return row // S == column // S
    return row % S == column % S


VMEM_LIMIT = pltpu.CompilerParams(vmem_limit_bytes=48 * 1024 * 1024)


def self_attend(qkv, spatial):
    rows = F * S

    def kernel(qkv_ref, out_ref):
        attend_heads(qkv_ref, qkv_ref, D, qkv_ref, 2 * D, out_ref, same_group(rows, spatial))

    return pl.pallas_call(
        kernel,
        grid=(qkv.shape[0] // rows,),
        in_specs=[pl.BlockSpec((rows, 3 * D), lambda i: (i, 0))],
        out_specs=pl.BlockSpec((rows, D), lambda i: (i, 0)),
        out_shape=jax.ShapeDtypeStruct((qkv.shape[0], D), jnp.bfloat16),
        compiler_params=VMEM_LIMIT,
        name="self_attend",
    )(qkv)


def self_attend_back(qkv, grad_mix, spatial):
    rows = F * S

    def kernel(qkv_ref, grad_ref, out_ref):
        attend_heads_back(
            qkv_ref, qkv_ref, D, qkv_ref, 2 * D, grad_ref,
            out_ref, out_ref, out_ref, same_group(rows, spatial),
        )

    return pl.pallas_call(
        kernel,
        grid=(qkv.shape[0] // rows,),
        in_specs=[
            pl.BlockSpec((rows, 3 * D), lambda i: (i, 0)),
            pl.BlockSpec((rows, D), lambda i: (i, 0)),
        ],
        out_specs=pl.BlockSpec((rows, 3 * D), lambda i: (i, 0)),
        out_shape=jax.ShapeDtypeStruct(qkv.shape, jnp.bfloat16),
        compiler_params=VMEM_LIMIT,
        name="self_attend_back",
    )(qkv, grad_mix)


def caption_mask(length):
    return lax.broadcasted_iota(jnp.int32, (F * S, LCAP), 1) < length


def cross_attend(query, pairs, lengths):
    clips = pairs.shape[0]

    def kernel(length_ref, query_ref, pair_ref, out_ref):
        allowed = caption_mask(length_ref[pl.program_id(0)])
        attend_heads(query_ref, pair_ref.at[0], 0, pair_ref.at[0], D, out_ref, allowed)

    return pl.pallas_call(
        kernel,
        grid_spec=pltpu.PrefetchScalarGridSpec(
            num_scalar_prefetch=1,
            grid=(clips,),
            in_specs=[
                pl.BlockSpec((F * S, D), lambda i, lens: (i, 0)),
                pl.BlockSpec((1, LCAP, 2 * D), lambda i, lens: (i, 0, 0)),
            ],
            out_specs=pl.BlockSpec((F * S, D), lambda i, lens: (i, 0)),
        ),
        out_shape=jax.ShapeDtypeStruct(query.shape, jnp.bfloat16),
        compiler_params=VMEM_LIMIT,
        name="cross_attend",
    )(lengths, query, pairs)


def cross_attend_back(query, pairs, grad_mix, lengths):
    clips = pairs.shape[0]

    def kernel(length_ref, query_ref, pair_ref, grad_ref, grad_query_ref, grad_pair_ref):
        allowed = caption_mask(length_ref[pl.program_id(0)])
        attend_heads_back(
            query_ref, pair_ref.at[0], 0, pair_ref.at[0], D, grad_ref,
            grad_query_ref, grad_pair_ref.at[0], grad_pair_ref.at[0], allowed,
        )

    return pl.pallas_call(
        kernel,
        grid_spec=pltpu.PrefetchScalarGridSpec(
            num_scalar_prefetch=1,
            grid=(clips,),
            in_specs=[
                pl.BlockSpec((F * S, D), lambda i, lens: (i, 0)),
                pl.BlockSpec((1, LCAP, 2 * D), lambda i, lens: (i, 0, 0)),
                pl.BlockSpec((F * S, D), lambda i, lens: (i, 0)),
            ],
            out_specs=[
                pl.BlockSpec((F * S, D), lambda i, lens: (i, 0)),
                pl.BlockSpec((1, LCAP, 2 * D), lambda i, lens: (i, 0, 0)),
            ],
        ),
        out_shape=[
            jax.ShapeDtypeStruct(query.shape, jnp.bfloat16),
            jax.ShapeDtypeStruct(pairs.shape, jnp.bfloat16),
        ],
        compiler_params=VMEM_LIMIT,
        name="cross_attend_back",
    )(lengths, query, pairs, grad_mix)


class Place:
    def __init__(self):
        self.wide = lax.axis_size("wide")
        self.narrow = lax.axis_size("narrow")
        self.depth = self.wide // 4
        self.half = self.depth // 2
        self.at = lax.axis_index("wide")
        self.core = self.at & 1
        self.x = (self.at >> 1) & 1
        self.z = self.at >> 2
        self.y = lax.axis_index("narrow")

    def over_wide(self, values, bit):
        return lax.ppermute(values, "wide", [(i, i ^ bit) for i in range(self.wide)])

    def over_core(self, values):
        return self.over_wide(values, 1)

    def over_x(self, values):
        return self.over_wide(values, 2)

    def over_z(self, values, bit):
        return self.over_wide(values, 4 * bit)

    def to_owner(self, values):
        pairs = [
            (i, i ^ 4 * self.half)
            for i in range(self.wide)
            if (i >> 2) // self.half != i & 1
        ]
        return lax.ppermute(values, "wide", pairs)

    def from_owner(self, values):
        pairs = [(i, i ^ 1) for i in range(self.wide) if (i >> 2) // self.half == i & 1]
        return lax.ppermute(values, "wide", pairs)

    def over_y(self, values, bit):
        return lax.ppermute(values, "narrow", [(i, i ^ bit) for i in range(self.narrow)])


def pair_up(bit, own, other):
    first = bit == 0
    return jnp.where(first, own, other), jnp.where(first, other, own)


def bits_of(size):
    return [1 << at for at in range(size.bit_length() - 1)]


def hold(values, others):
    if not others:
        return values
    kept, _ = lax.optimization_barrier((values, others))
    return kept


class Ticks:
    def __init__(self, joint):
        self.joint = joint
        self.ended = {True: [], False: []}
        self.sent = []

    def run(self, jobs, others=()):
        self.before = self.ended[True]
        ended = {True: [], False: []}
        before = dict(self.ended)
        if self.joint:
            before = {kind: list(before.values()) for kind in before}
            self.ended = {True: [], False: []}
        self.sent = []
        results = []
        for kind in (True, False):
            mine = [job for job in jobs if job.planar == kind]
            if not mine:
                continue
            values = [[value for value, _ in job.sends] for job in mine]
            values = hold(values, [before[kind], list(others)])
            self.sent.append(values)
            for job, held in zip(mine, values):
                result = [exchange(value) for value, (_, exchange) in zip(held, job.sends)]
                ended[kind].append(result)
                results.append((job, result))
            self.ended[kind] = ended[kind]
        for job, result in results:
            job.take(result)

    def during(self, values):
        return hold(values, [self.sent, self.before])

    def after(self, values):
        return hold(values, self.ended[True])


class Job:
    planar = False

    def __init__(self, transfers):
        self.transfers = transfers
        self.sends = next(transfers)

    def take(self, results):
        try:
            self.sends = self.transfers.send(results)
        except StopIteration:
            self.sends = None


def spread_y(place, values):
    pieces = [values]
    for bit in bits_of(place.narrow):
        pieces = pieces + [place.over_y(piece, bit) for piece in pieces]
    return pieces[1:]


class Gather(Job):
    def __init__(self, place, own):
        self.place = place
        super().__init__(self.plan(own[None]))

    def plan(self, block):
        place = self.place
        half = place.half
        rows, width = block.shape[1:]
        self.folded = place.narrow == 2 and width % 128 != 0 and rows % 16 == 0
        if self.folded:
            block = jnp.concatenate([block[:, : rows // 2], block[:, rows // 2 :]], axis=-1)
        for bit in bits_of(half):
            [other] = yield [(block, lambda values, bit=bit: place.over_z(values, bit))]
            block = jnp.concatenate(pair_up(place.z & bit, block, other))
        quarter = half // 2
        low, high = block[:quarter], block[quarter:]
        [low_away] = yield [(low, lambda values: place.over_z(values, half))]
        [high_away] = yield [(high, lambda values: place.over_z(values, half))]
        low = pair_up(place.z & half, low, low_away)
        high = pair_up(place.z & half, high, high_away)
        block = jnp.concatenate([low[0], high[0], low[1], high[1]])
        self.planar = True
        by_x, by_y = yield [(block, place.over_x), (block, lambda values: spread_y(place, values))]
        far_xy, near_xy = yield [
            (jnp.stack([piece[half:] for piece in by_y]), place.over_x),
            (by_x[:half], lambda values: spread_y(place, values)),
        ]
        columns = width * place.narrow
        mine = unwritten((place.depth, 2, rows, columns))
        parts = (
            (0, 0, self.lanes([block] + list(by_y))),
            (0, 1, self.lanes([by_x[:half]] + list(near_xy))),
            (half, 1, self.lanes([by_x[half:]] + [far_xy[at] for at in range(place.narrow - 1)])),
        )
        for first_z, apart, part in parts:
            mine = lax.dynamic_update_slice(
                mine, part[:, None], (first_z, place.x ^ apart, 0, 0)
            )
        self.mine = mine
        self.planar = False
        [self.other] = yield [(mine, place.over_core)]

    def lanes(self, pieces):
        place = self.place
        if place.narrow == 1:
            return pieces[0]
        if self.folded:
            low, high = pair_up(place.y, pieces[0], pieces[1])
            width = low.shape[-1] // 2
            return jnp.concatenate(
                [
                    jnp.concatenate([low[..., :width], high[..., :width]], axis=-1),
                    jnp.concatenate([low[..., width:], high[..., width:]], axis=-1),
                ],
                axis=-2,
            )
        if place.narrow == 2:
            return jnp.concatenate(pair_up(place.y, pieces[0], pieces[1]), axis=-1)
        return jnp.concatenate(
            [lax.select_n(place.y ^ spot, *pieces) for spot in range(place.narrow)], axis=-1
        )

    def whole(self, first_row, rows):
        place = self.place
        span = slice(first_row, first_row + rows)
        columns = self.mine.shape[-1]
        whole = unwritten((place.depth, 2, 2, rows, columns))
        for part, core in ((self.mine, place.core), (self.other, 1 - place.core)):
            whole = lax.dynamic_update_slice(
                whole, part[:, :, None, span], (0, 0, core, 0, 0)
            )
        return whole.reshape(place.wide * rows, columns)


def unwritten(shape):
    return pl.pallas_call(
        lambda out_ref: None,
        out_specs=pl.BlockSpec(memory_space=pl.ANY),
        out_shape=jax.ShapeDtypeStruct(shape, jnp.bfloat16),
        name="unwritten",
    )()


def side(values, bit, axis):
    return lax.dynamic_index_in_dim(values, bit, axis, keepdims=False)


def columns_at(values, index, count):
    width = values.shape[-1] // count
    if count == 1:
        return values
    if count == 2:
        return jnp.where(index == 0, values[..., :width], values[..., width:])
    return lax.dynamic_slice_in_dim(values, index * width, width, axis=values.ndim - 1)


def wide_float(values):
    return values.astype(jnp.float32)


def reduce_y(place, values):
    for bit in reversed(bits_of(place.narrow)):
        upper = ((place.y & bit) != 0).astype(jnp.int32)
        away = place.over_y(rounded(columns_at(values, 1 - upper, 2)), bit)
        values = columns_at(values, upper, 2) + wide_float(away)
    return values


class Scatter(Job):
    def __init__(self, place, products):
        self.place = place
        super().__init__(self.plan(products))

    def plan(self, products):
        place = self.place
        spread = place.half
        quarter = spread // 2
        sends = [(grad, place.over_core) for _, _, grad, *known in products if len(known) == 1]
        away = iter((yield sends) if sends else ())
        views = []
        for operand, operand_away, grad, parts, *known in products:
            grad_away = known[0] if known else next(away)
            kept = matmul_tn(columns_at(operand, place.core, 2), grad)
            total = matmul_tn(columns_at(operand_away, place.core, 2), grad_away)
            total = rounded(total + wide_float(rounded(kept)))
            width = grad.shape[1] // parts
            for part in range(parts):
                view = total[:, part * width : (part + 1) * width]
                views.append(view.reshape(spread, 2, -1, width))

        def summed(span, x_bit=None):
            mine = [view[span] for view in views]
            if x_bit is not None:
                mine = [side(view, x_bit, 1) for view in mine]
            return jnp.concatenate(mine, axis=-2) if len(mine) > 1 else mine[0]

        near_span, far_span = slice(0, quarter), slice(quarter, None)
        self.planar = True
        if place.narrow == 2:
            near_away, far_away = yield [
                (summed(near_span, 1 - place.x), place.over_x),
                (
                    columns_at(summed(far_span), 1 - place.y, 2),
                    lambda values: place.over_y(values, 1),
                ),
            ]

            def near(y_bit):
                mine = columns_at(summed(near_span, place.x), y_bit, 2)
                return wide_float(mine) + wide_float(columns_at(near_away, y_bit, 2))

            def far(x_bit):
                mine = columns_at(summed(far_span, x_bit), place.y, 2)
                return wide_float(mine) + wide_float(side(far_away, x_bit, 1))

            near_back, far_back = yield [
                (rounded(near(1 - place.y)), lambda values: place.over_y(values, 1)),
                (rounded(far(1 - place.x)), place.over_x),
            ]
            near = near(place.y) + wide_float(near_back)
            far = far(place.x) + wide_float(far_back)
        else:
            near_away, far = yield [
                (summed(near_span, 1 - place.x), place.over_x),
                (wide_float(summed(far_span)), lambda values: reduce_y(place, values)),
            ]
            near = wide_float(summed(near_span, place.x)) + wide_float(near_away)
            near, far_back = yield [
                (near, lambda values: reduce_y(place, values)),
                (rounded(side(far, 1 - place.x, 1)), place.over_x),
            ]
            far = side(far, place.x, 1) + wide_float(far_back)
        self.planar = False
        total, sent = pair_up(place.z & quarter, near, far)
        [away] = yield [(rounded(sent), lambda values: place.over_z(values, quarter))]
        total = total + wide_float(away)
        for bit in reversed(bits_of(quarter)):
            total = total.reshape((2, total.shape[0] // 2) + total.shape[1:])
            upper = ((place.z & bit) != 0).astype(jnp.int32)
            [away] = yield [
                (
                    rounded(side(total, 1 - upper, 0)),
                    lambda values, bit=bit: place.over_z(values, bit),
                )
            ]
            total = side(total, upper, 0) + wide_float(away)
        total = total[0]
        [away] = yield [(rounded(total), place.to_owner)]
        total = total + wide_float(away)
        pieces, first = [], 0
        for view in views:
            rows = view.shape[2]
            pieces.append(total[first : first + rows].reshape(2, rows // 2, -1))
            first += rows
        sent = [side(piece, 1 - place.core, 0) for piece in pieces]
        sent = jnp.concatenate(sent) if len(sent) > 1 else sent[0]
        [away] = yield [(sent, place.from_owner)]
        owner = place.z // spread == place.core
        self.total, first = [], 0
        for piece in pieces:
            rows = piece.shape[1]
            theirs = away[first : first + rows]
            self.total.append(jnp.where(owner, side(piece, place.core, 0), theirs))
            first += rows


class Reducer:
    def __init__(self, place):
        self.place = place
        self.ticks = Ticks(False)
        self.jobs = []

    def add(self, *products):
        job = Scatter(self.place, products)
        self.jobs.append(job)
        return job

    def run(self, *others, wait=()):
        due = [job for job in self.jobs if job.sends is not None and job not in wait]
        if due:
            self.ticks.run(due, others)
        return bool(due)


def adam_update(master, first_moment, second_moment, gradient, step_value):
    first_new = 0.9 * first_moment + 0.1 * gradient
    second_new = 0.999 * second_moment + 0.001 * gradient * gradient
    first_hat = first_new / (1.0 - 0.9**step_value)
    second_hat = second_new / (1.0 - 0.999**step_value)
    master_new = master - LEARNING_RATE * (
        first_hat / (jnp.sqrt(second_hat) + 1e-08) + 0.01 * master
    )
    return (master_new, first_new, second_new)


def body(
    projections,
    qkv_weights,
    mlp_weights,
    ada_weights,
    entry_weights,
    patch_weights,
    shift_tables,
    first_projections,
    first_qkv_weights,
    first_mlp_weights,
    first_ada_weights,
    first_entry_weights,
    first_patch_weights,
    first_shift_tables,
    second_projections,
    second_qkv_weights,
    second_mlp_weights,
    second_ada_weights,
    second_entry_weights,
    second_patch_weights,
    second_shift_tables,
    latents,
    noise,
    captions,
    cap_len,
    timesteps,
    step_count,
):
    shards = (
        projections,
        qkv_weights,
        mlp_weights,
        ada_weights,
        entry_weights,
        patch_weights,
        shift_tables,
    )
    firsts = (
        first_projections,
        first_qkv_weights,
        first_mlp_weights,
        first_ada_weights,
        first_entry_weights,
        first_patch_weights,
        first_shift_tables,
    )
    seconds = (
        second_projections,
        second_qkv_weights,
        second_mlp_weights,
        second_ada_weights,
        second_entry_weights,
        second_patch_weights,
        second_shift_tables,
    )
    place = Place()
    clips = latents.shape[0]
    tokens = F * S
    video_count = clips * place.wide * place.narrow
    rows = projections.shape[1]
    entry_rows = entry_weights.shape[0]

    def by_clip(values):
        return values.reshape(clips, tokens, values.shape[-1])

    def flat(values):
        return values.reshape(clips * tokens, values.shape[-1])

    devices = place.wide * place.narrow
    all_clips = clips * devices

    def to_all(values):
        return lax.all_to_all(values, ("wide", "narrow"), split_axis=0, concat_axis=0, tiled=True)

    def columns_to_all(values):
        pieces = values.reshape(values.shape[0], place.narrow, -1).transpose(1, 0, 2)
        pieces = jnp.broadcast_to(pieces[None], (place.wide,) + pieces.shape)
        return to_all(pieces.reshape((devices,) + pieces.shape[2:]))

    proj_low, qkv_low, mlp_low, ada_low, entry_low, patch_low, table_low = (
        rounded(shard) for shard in shards
    )
    width = projections.shape[2]
    small = jnp.concatenate([patch_low.reshape(-1), table_low.reshape(-1)])
    small_rows = -(-small.shape[0] // (8 * width)) * 8
    small = jnp.pad(small, (0, small_rows * width - small.shape[0])).reshape(small_rows, width)
    ticks = Ticks(True)
    gathers = [
        Gather(place, own)
        for own in (
            jnp.concatenate([proj_low[:2].reshape(2 * rows, width), small]),
            entry_low,
            qkv_low.reshape(2 * rows, -1),
            proj_low[2:].reshape(6 * rows, width),
            mlp_low[0],
            mlp_low[1],
        )
    ]
    early, entry_gather, qkv_gather, late, mlp_in_gather, mlp_out_gather = gathers
    rounds = iter(range(2 * len(gathers) + len(bits_of(place.depth)) + 4))

    def gather_on(*others):
        now = next(rounds)
        due = [job for at, job in enumerate(gathers) if job.sends is not None and now >= 2 * at]
        if due:
            ticks.run(due, others)

    while early.sends is not None:
        gather_on()
    small_all = early.whole(2 * rows, small_rows)
    proj_all = [early.whole(0, rows), early.whole(rows, rows)]
    small_all = small_all.reshape(place.wide, small_rows, place.narrow, width).transpose(0, 2, 1, 3)
    small_all = small_all.reshape(place.wide, place.narrow, small_rows * width)
    patch_count = patch_low.size
    patch_all = small_all[:, :, :patch_count].reshape(
        (place.wide, place.narrow) + patch_low.shape
    )
    patch_all = patch_all.transpose(2, 0, 3, 1, 4).reshape(2, D, -1)
    table_all = small_all[:, :, patch_count : patch_count + table_low.size].reshape(
        (place.wide, place.narrow) + table_low.shape
    )
    table_all = table_all.transpose(1, 2, 0, 3).reshape(8, D).astype(jnp.float32)

    time_value = timesteps.astype(jnp.float32)
    signal = jnp.cos((time_value / 1000.0 + 0.008) / 1.008 * (math.pi / 2)) ** 2
    noise_rows = flat(noise.astype(jnp.float32))
    noised_low = rounded(
        flat(
            jnp.sqrt(signal)[:, None, None] * latents.astype(jnp.float32)
            + jnp.sqrt(1.0 - signal)[:, None, None] * noise.astype(jnp.float32)
        )
    )
    spatial_pos = jnp.tile(sinusoid(jnp.arange(S, dtype=jnp.float32), D), (clips * F, 1))
    frame_pos = jnp.tile(jnp.repeat(sinusoid(jnp.arange(F, dtype=jnp.float32), D), S, 0), (clips, 1))
    embed_low = rounded(sinusoid(time_value, FREQ))
    while entry_gather.sends is not None:
        gather_on(patch_all, table_all)
    gather_on()
    entry_gather.other = ticks.during(entry_gather.other)
    entry_all = entry_gather.whole(0, entry_rows)
    time_inner = matmul(embed_low, entry_all[CAP:])
    inner_low = rounded(jax.nn.silu(time_inner))
    time_embed = matmul(inner_low, proj_all[0])
    embed_act = rounded(jax.nn.silu(time_embed))

    def by_rows(values):
        return values.reshape(clips, place.wide, rows).transpose(1, 0, 2)

    sent = jnp.concatenate(
        [
            by_rows(embed_act),
            by_rows(inner_low),
            jnp.broadcast_to(embed_low[None], (place.wide,) + embed_low.shape),
        ],
        axis=-1,
    )
    sent = jnp.broadcast_to(sent[:, None], (place.wide, place.narrow) + sent.shape[1:])
    gather_on(sent, entry_all)
    sent = ticks.during(sent)
    sent = to_all(sent.reshape((devices,) + sent.shape[2:])).reshape(all_clips, -1)
    my_embed_act, my_inner, embed_all = sent[:, :rows], sent[:, rows : 2 * rows], sent[:, 2 * rows :]
    part = matmul(my_embed_act, ada_low).reshape(devices, clips, -1)

    caption_rows = captions.reshape(clips * LCAP, CAP)
    caption_wide = jnp.pad(caption_rows, ((0, 0), (0, place.wide * entry_rows - CAP)))
    caption_inner = matmul(ticks.during(caption_rows), entry_all[:CAP])
    caption_act = rounded(jax.nn.gelu(caption_inner))
    context_low = rounded(matmul(caption_act, proj_all[1]))
    gather_on(context_low, part)
    part = to_all(ticks.during(part))
    qkv_gather.other = ticks.during(qkv_gather.other)
    qkv_all = [qkv_gather.whole(0, rows), qkv_gather.whole(rows, rows)]
    part = part.reshape(place.wide, place.narrow, clips, -1)
    modulations = jnp.sum(part, axis=0).transpose(1, 0, 2).reshape(clips, 6, D) + table_all[:6]
    caption_wide_away = place.over_core(caption_wide)
    caption_act_away = place.over_core(caption_act)
    context_low_away = place.over_core(context_low)
    gather_on(modulations, caption_wide_away, caption_act_away, context_low_away, *qkv_all)
    modulations = ticks.during(modulations)
    shift_a, scale_a, gate_a, shift_m, scale_m, gate_m = (
        modulations[:, at : at + 1] for at in range(6)
    )
    final_shift = (time_embed + table_all[6])[:, None]
    final_scale = (time_embed + table_all[7])[:, None]

    hidden = matmul_nt(noised_low, patch_all[0]) + spatial_pos
    normed_spatial = rounded(flat(modulate(by_clip(hidden), shift_a, scale_a)))
    spatial_qkv = rounded(matmul(normed_spatial, qkv_all[0]))
    normed_spatial_away = place.over_core(normed_spatial)
    gather_on(spatial_qkv, normed_spatial_away)
    late.other = ticks.during(late.other)
    proj_all = proj_all + [late.whole(at * rows, rows) for at in range(6)]
    pair_weight = jnp.concatenate([proj_all[5], proj_all[6]], axis=1)
    spatial_mix = self_attend(ticks.during(spatial_qkv), True)
    gather_on(spatial_mix, pair_weight, *proj_all)
    spatial_mix, context_low = ticks.during((spatial_mix, context_low))
    cross_pairs = rounded(matmul(context_low, pair_weight))
    spatial_out = matmul(spatial_mix, proj_all[2])
    hidden_one = hidden + flat(gate_a * by_clip(spatial_out))
    temporal_in = rounded(hidden_one + frame_pos)
    temporal_qkv = rounded(matmul(temporal_in, qkv_all[1]))
    spatial_mix_away = place.over_core(spatial_mix)
    temporal_in_away = place.over_core(temporal_in)
    gather_on(cross_pairs, temporal_qkv, spatial_mix_away, temporal_in_away)
    temporal_mix = self_attend(ticks.during(temporal_qkv), False)
    mlp_in_gather.other = ticks.during(mlp_in_gather.other)
    mlp_in = mlp_in_gather.whole(0, rows)
    temporal_out = matmul(temporal_mix, proj_all[3])
    hidden_two = hidden_one + flat(gate_a * by_clip(temporal_out))
    hidden_two_low = rounded(hidden_two)
    temporal_mix_away = place.over_core(temporal_mix)
    hidden_two_low_away = place.over_core(hidden_two_low)
    cross_query = rounded(matmul(hidden_two_low, proj_all[4]))
    while mlp_out_gather.sends is not None:
        gather_on(cross_query, mlp_in)
    mlp_out = mlp_out_gather.whole(0, rows)
    cross_mix = cross_attend(cross_query, cross_pairs.reshape(clips, LCAP, 2 * D), cap_len)
    cross_mix_away = place.over_core(cross_mix)
    hidden_three = hidden_two + matmul(cross_mix, proj_all[7])
    normed_mlp = rounded(flat(modulate(by_clip(hidden_three), shift_m, scale_m)))
    normed_mlp_away = place.over_core(normed_mlp)
    expand = matmul(normed_mlp, mlp_in)
    expand_act = rounded(jax.nn.gelu(expand))
    expand_act_away = place.over_core(expand_act)
    contract = matmul_nt(expand_act, mlp_out)
    hidden_four = hidden_three + flat(gate_m * by_clip(contract))
    final_low = rounded(flat(modulate(by_clip(hidden_four), final_shift, final_scale)))
    misfit = matmul(final_low, patch_all[1]) - noise_rows
    entries = tokens * latents.shape[2]
    loss_value = jnp.sum(misfit * misfit) / (entries * video_count)

    grad_pred = rounded(2.0 * misfit / (entries * video_count))
    grad_patch_out = matmul_tn(final_low, grad_pred)
    _, pull_final = jax.vjp(modulate, by_clip(hidden_four), final_shift, final_scale)
    grad_four, grad_fshift, grad_fscale = pull_final(by_clip(matmul_nt(grad_pred, patch_all[1])))
    grad_contract = rounded(flat(grad_four * gate_m))
    grad_gate_mlp = jnp.sum(grad_four * by_clip(contract), axis=1)
    reducer = Reducer(place)
    during, after = reducer.ticks.during, reducer.ticks.after
    grad_contract_away = place.over_core(grad_contract)
    mlp_out_scatter = reducer.add(
        (grad_contract, grad_contract_away, expand_act, 1, expand_act_away)
    )
    reducer.run()
    _, pull_gelu = jax.vjp(jax.nn.gelu, expand)
    grad_expand = rounded(pull_gelu(matmul(during(grad_contract), mlp_out))[0])
    mlp_in_scatter = reducer.add((normed_mlp, normed_mlp_away, grad_expand, 1))
    reducer.run()
    _, pull_mlp_norm = jax.vjp(modulate, by_clip(hidden_three), shift_m, scale_m)
    grad_three_part, grad_shift_mlp, grad_scale_mlp = pull_mlp_norm(
        by_clip(matmul_nt(during(grad_expand), mlp_in))
    )
    grad_three = flat(grad_four + grad_three_part)
    grad_cross_out = rounded(grad_three)
    reducer.run(grad_cross_out)
    grad_cross_mix = rounded(matmul_nt(during(grad_cross_out), proj_all[7]))
    grad_query_low, grad_pairs_low = cross_attend_back(
        cross_query, cross_pairs.reshape(clips, LCAP, 2 * D), grad_cross_mix, cap_len
    )
    grad_pairs_low = grad_pairs_low.reshape(clips * LCAP, 2 * D)
    grad_context = rounded(matmul_nt(grad_pairs_low, pair_weight))
    caption_scatter = reducer.add(
        (caption_act, caption_act_away, grad_context, 1),
        (context_low, context_low_away, grad_pairs_low, 2),
    )
    reducer.run(grad_query_low)
    _, pull_caption = jax.vjp(jax.nn.gelu, caption_inner)
    grad_context, grad_query_low = during((grad_context, grad_query_low))
    grad_caption_inner = rounded(pull_caption(matmul_nt(grad_context, proj_all[1]))[0])
    grad_two = grad_three + matmul_nt(grad_query_low, proj_all[4])
    grad_temporal_out = rounded(flat(by_clip(grad_two) * gate_a))
    grad_gate_attn = jnp.sum(by_clip(grad_two * temporal_out), axis=1)
    grad_temporal_mix = rounded(matmul_nt(grad_temporal_out, proj_all[3]))
    reducer.run(grad_temporal_mix, grad_caption_inner)
    grad_temporal_qkv = self_attend_back(temporal_qkv, during(grad_temporal_mix), False)
    entry_scatter = reducer.add((caption_wide, caption_wide_away, grad_caption_inner, 1))
    qkv_one_scatter = reducer.add((temporal_in, temporal_in_away, grad_temporal_qkv, 1))
    reducer.run()
    grad_one = grad_two + matmul_nt(during(grad_temporal_qkv), qkv_all[1])
    grad_spatial_out = rounded(flat(by_clip(grad_one) * gate_a))
    grad_gate_attn = grad_gate_attn + jnp.sum(by_clip(grad_one * spatial_out), axis=1)
    grad_spatial_mix = rounded(matmul_nt(grad_spatial_out, proj_all[2]))
    reducer.run(grad_spatial_mix, wait=(qkv_one_scatter,))
    grad_spatial_qkv = self_attend_back(spatial_qkv, during(grad_spatial_mix), True)
    qkv_zero_scatter = reducer.add((normed_spatial, normed_spatial_away, grad_spatial_qkv, 1))
    reducer.run(wait=(qkv_one_scatter,))
    grad_normed_spatial = matmul_nt(during(grad_spatial_qkv), qkv_all[0])
    square_scatter = reducer.add(
        (spatial_mix, spatial_mix_away, grad_spatial_out, 1),
        (temporal_mix, temporal_mix_away, grad_temporal_out, 1),
        (hidden_two_low, hidden_two_low_away, grad_query_low, 1),
        (cross_mix, cross_mix_away, grad_cross_out, 1),
    )
    reducer.run(grad_normed_spatial, wait=(qkv_zero_scatter,))
    grad_normed_spatial = during(grad_normed_spatial)
    reducer.run(wait=(qkv_zero_scatter, square_scatter))
    reducer.run(wait=(square_scatter,))
    qkv_zero_started = reducer.ticks.sent
    reducer.run(wait=(square_scatter,))
    reducer.run()
    middle = reducer.ticks.sent
    while reducer.run():
        pass
    sum_mlp_in, sum_mlp_out = mlp_in_scatter.total[0], mlp_out_scatter.total[0]
    sum_qkv_one = qkv_one_scatter.total[0]
    sum_qkv_zero = qkv_zero_scatter.total[0]
    sum_two, sum_three, sum_four, sum_seven = square_scatter.total
    sum_one, sum_five, sum_six = caption_scatter.total
    sum_entry = entry_scatter.total[0]
    _, pull_spatial_norm = jax.vjp(modulate, by_clip(hidden), shift_a, scale_a)
    grad_hidden_part, grad_shift_attn, grad_scale_attn = pull_spatial_norm(
        by_clip(grad_normed_spatial)
    )
    grad_hidden = rounded(grad_one + flat(grad_hidden_part))
    grad_patch_in = matmul_tn(grad_hidden, noised_low)
    grad_modulations = jnp.stack(
        [
            grad_shift_attn[:, 0],
            grad_scale_attn[:, 0],
            grad_gate_attn,
            grad_shift_mlp[:, 0],
            grad_scale_mlp[:, 0],
            grad_gate_mlp,
        ],
        axis=1,
    )

    grad_ada_out = hold(rounded(grad_modulations.reshape(clips, 6 * D)), qkv_zero_started)
    grad_ada_mine = columns_to_all(grad_ada_out).reshape(all_clips, -1)
    grad_ada = matmul_tn(my_embed_act, grad_ada_mine)
    grad_ada_mine = hold(grad_ada_mine, middle)
    act_part = to_all(matmul_nt(grad_ada_mine, ada_low).reshape(devices, clips, rows))
    act_part = jnp.sum(act_part.reshape(place.wide, place.narrow, clips, rows), axis=1)
    grad_embed_act = act_part.transpose(1, 0, 2).reshape(clips, D)
    _, pull_embed = jax.vjp(jax.nn.silu, time_embed)
    grad_time_embed = rounded(
        pull_embed(grad_embed_act)[0] + (grad_fshift + grad_fscale)[:, 0]
    )
    _, pull_inner = jax.vjp(jax.nn.silu, time_inner)
    grad_time_inner = rounded(pull_inner(matmul_nt(grad_time_embed, proj_all[0]))[0])
    time_rows = columns_to_all(jnp.concatenate([grad_time_embed, grad_time_inner]))
    grad_embed_mine = time_rows[:, :clips].reshape(all_clips, width)
    grad_inner_mine = time_rows[:, clips:].reshape(all_clips, width)
    grad_proj_zero = matmul_tn(my_inner, grad_embed_mine)
    grad_time_rows = matmul_tn(embed_all, grad_inner_mine)
    spot = jnp.clip((place.at + 1) * entry_rows - CAP, 0, FREQ + entry_rows)
    padded_rows = jnp.pad(grad_time_rows, ((entry_rows, entry_rows), (0, 0)))
    grad_entry_time = lax.dynamic_slice_in_dim(padded_rows, spot, entry_rows, axis=0)

    grad_tables = jnp.concatenate(
        [
            jnp.sum(grad_modulations, axis=0),
            jnp.sum(grad_fshift, axis=0),
            jnp.sum(grad_fscale, axis=0),
        ]
    )
    grad_patches = jnp.stack([grad_patch_in, grad_patch_out]).reshape(
        2, place.wide, rows, place.narrow, -1
    )
    grad_tables = grad_tables.reshape(place.narrow, -1, place.wide, rows)
    small_grads = jnp.concatenate(
        [
            grad_patches.transpose(1, 3, 0, 2, 4).reshape(devices, -1),
            grad_tables.transpose(2, 0, 1, 3).reshape(devices, -1),
        ],
        axis=1,
    )
    small_grads = jnp.sum(to_all(hold(small_grads, middle)), axis=0)
    sum_patch = small_grads[: patch_weights.size].reshape(patch_weights.shape)
    sum_tables = small_grads[patch_weights.size :].reshape(shift_tables.shape)

    sum_projections = jnp.stack(
        [
            grad_proj_zero,
            sum_one,
            sum_two,
            sum_three,
            sum_four,
            sum_five,
            sum_six,
            sum_seven,
        ]
    )
    summed = (
        sum_projections,
        jnp.stack([sum_qkv_zero, sum_qkv_one]),
        jnp.stack([sum_mlp_in, sum_mlp_out]),
        grad_ada,
        sum_entry + grad_entry_time,
        sum_patch,
        sum_tables,
    )
    square_part = sum((jnp.sum(piece * piece) for piece in summed))
    both = jnp.broadcast_to(jnp.stack([loss_value, square_part]), (devices, 2))
    loss_total, square_total = jnp.sum(to_all(both), axis=0)
    grad_norm = jnp.sqrt(square_total)
    threshold = (video_count * latents.shape[1]) ** (-0.5)
    factor = threshold / jnp.maximum(grad_norm, threshold)
    step_value = step_count[0].astype(jnp.float32)
    updated = [
        adam_update(master, first_moment, second_moment, gradient * factor, step_value)
        for master, first_moment, second_moment, gradient in zip(shards, firsts, seconds, summed)
    ]
    return (
        updated[0][0],
        updated[1][0],
        updated[2][0],
        updated[3][0],
        updated[4][0],
        updated[5][0],
        updated[6][0],
        updated[0][1],
        updated[1][1],
        updated[2][1],
        updated[3][1],
        updated[4][1],
        updated[5][1],
        updated[6][1],
        updated[0][2],
        updated[1][2],
        updated[2][2],
        updated[3][2],
        updated[4][2],
        updated[5][2],
        updated[6][2],
        loss_total,
        grad_norm,
    )


def solution(mesh):
    return jax.shard_map(
        body,
        mesh=mesh,
        in_specs=(
            P(None, "wide", "narrow"),
            P(None, "wide", "narrow"),
            P(None, "wide", "narrow"),
            P("wide", "narrow"),
            P("wide", "narrow"),
            P(None, "wide", "narrow"),
            P("narrow", "wide"),
            P(None, "wide", "narrow"),
            P(None, "wide", "narrow"),
            P(None, "wide", "narrow"),
            P("wide", "narrow"),
            P("wide", "narrow"),
            P(None, "wide", "narrow"),
            P("narrow", "wide"),
            P(None, "wide", "narrow"),
            P(None, "wide", "narrow"),
            P(None, "wide", "narrow"),
            P("wide", "narrow"),
            P("wide", "narrow"),
            P(None, "wide", "narrow"),
            P("narrow", "wide"),
            P(("wide", "narrow"), None, None),
            P(("wide", "narrow"), None, None),
            P(("wide", "narrow"), None, None),
            P(("wide", "narrow")),
            P(("wide", "narrow")),
            P(),
        ),
        out_specs=(
            P(None, "wide", "narrow"),
            P(None, "wide", "narrow"),
            P(None, "wide", "narrow"),
            P("wide", "narrow"),
            P("wide", "narrow"),
            P(None, "wide", "narrow"),
            P("narrow", "wide"),
            P(None, "wide", "narrow"),
            P(None, "wide", "narrow"),
            P(None, "wide", "narrow"),
            P("wide", "narrow"),
            P("wide", "narrow"),
            P(None, "wide", "narrow"),
            P("narrow", "wide"),
            P(None, "wide", "narrow"),
            P(None, "wide", "narrow"),
            P(None, "wide", "narrow"),
            P("wide", "narrow"),
            P("wide", "narrow"),
            P(None, "wide", "narrow"),
            P("narrow", "wide"),
            P(),
            P(),
        ),
        check_vma=False,
    )
```

```python
import math

import jax
import jax.numpy as jnp
from jax import lax
from jax.experimental import pallas as pl
from jax.experimental.pallas import tpu as pltpu
from jax.sharding import PartitionSpec as P

D = 1152
HEADS = 16
HEAD_DIM = 72
CAP = 4096
FREQ = 256
F = 16
S = 16
LCAP = 120


LEARNING_RATE = 0.04


def rounded(values):
    return values.astype(jnp.bfloat16)


def matmul(operand, matrix):
    return jnp.dot(operand, matrix, preferred_element_type=jnp.float32)


def matmul_tn(operand, matrix):
    return lax.dot_general(
        operand, matrix, (((0,), (0,)), ((), ())), preferred_element_type=jnp.float32
    )


def matmul_nt(operand, matrix):
    return lax.dot_general(
        operand, matrix, (((1,), (1,)), ((), ())), preferred_element_type=jnp.float32
    )


def sinusoid(places, feature):
    half_width = feature // 2
    freqs_row = jnp.exp(-math.log(10000.0) * jnp.arange(half_width, dtype=jnp.float32) / half_width)
    angles = places[:, None] * freqs_row[None, :]
    return jnp.concatenate([jnp.cos(angles), jnp.sin(angles)], axis=1)


def layer_norm(values):
    centred = values - jnp.mean(values, axis=-1, keepdims=True)
    return centred * lax.rsqrt(jnp.mean(centred * centred, axis=-1, keepdims=True) + 1e-06)


def modulate(values, shift_row, scale_row):
    return layer_norm(values) * (1.0 + scale_row) + shift_row


def head_window(head):
    first = HEAD_DIM * head
    low_lane = first // 128 * 128
    high_lane = -(-(first + HEAD_DIM) // 128) * 128
    return (first - low_lane, low_lane, high_lane)


def lanes_of_head(rows, head):
    offset, low_lane, high_lane = head_window(head)
    lane = lax.broadcasted_iota(jnp.int32, (rows, high_lane - low_lane), 1)
    return (lane >= offset) & (lane < offset + HEAD_DIM)


def dot_f32(left, right, contract):
    return lax.dot_general(
        left, right, ((contract[:1], contract[1:]), ((), ())), preferred_element_type=jnp.float32
    )


def softmax_rows(scores, allowed):
    scores = jnp.where(allowed, scores * HEAD_DIM ** (-0.5), -1000000000.0)
    powers = jnp.exp(scores - jnp.max(scores, axis=-1, keepdims=True))
    return powers * (1.0 / jnp.sum(powers, axis=-1, keepdims=True))


class HeadSums:
    def __init__(self, ref, base):
        self.ref = ref
        self.base = base
        self.tiles = {}

    def add(self, head, values):
        _, low_lane, high_lane = head_window(head)
        for tile in range(low_lane // 128, high_lane // 128):
            start = 128 * tile - low_lane
            share = values[:, start : start + 128]
            self.tiles[tile] = self.tiles[tile] + share if tile in self.tiles else share
        done = D // 128 if head == HEADS - 1 else HEAD_DIM * (head + 1) // 128
        for tile in [at for at in self.tiles if at < done]:
            start = self.base + 128 * tile
            self.ref[:, start : start + 128] = self.tiles.pop(tile).astype(self.ref.dtype)


def head_lanes(ref, base, head):
    _, low_lane, high_lane = head_window(head)
    values = ref[:, base + low_lane : base + high_lane]
    return jnp.where(lanes_of_head(values.shape[0], head), values, jnp.zeros_like(values))


def attend_heads(query_ref, key_ref, key_base, value_ref, value_base, out_ref, allowed):
    sums = HeadSums(out_ref, 0)
    for head in range(HEADS):
        _, low_lane, high_lane = head_window(head)
        query = head_lanes(query_ref, 0, head)
        key = key_ref[:, key_base + low_lane : key_base + high_lane]
        weights = softmax_rows(dot_f32(query, key, (1, 1)), allowed)
        value = head_lanes(value_ref, value_base, head)
        sums.add(head, dot_f32(rounded(weights), value, (1, 0)))


def attend_heads_back(
    query_ref, key_ref, key_base, value_ref, value_base, grad_ref,
    grad_query_ref, grad_key_ref, grad_value_ref, allowed,
):
    query_sums = HeadSums(grad_query_ref, 0)
    key_sums = HeadSums(grad_key_ref, key_base)
    value_sums = HeadSums(grad_value_ref, value_base)
    for head in range(HEADS):
        _, low_lane, high_lane = head_window(head)
        query = head_lanes(query_ref, 0, head)
        key = head_lanes(key_ref, key_base, head)
        value = value_ref[:, value_base + low_lane : value_base + high_lane]
        grad = head_lanes(grad_ref, 0, head)
        weights = softmax_rows(dot_f32(query, key, (1, 1)), allowed)
        grad_weights = dot_f32(grad, value, (1, 1))
        value_sums.add(head, dot_f32(rounded(weights), grad, (0, 0)))
        grad_scores = weights * (
            grad_weights - jnp.sum(grad_weights * weights, axis=-1, keepdims=True)
        )
        grad_low = rounded(grad_scores * HEAD_DIM ** (-0.5))
        query_sums.add(head, dot_f32(grad_low, key, (1, 0)))
        key_sums.add(head, dot_f32(grad_low, query, (0, 0)))


def same_group(rows, spatial):
    row = lax.broadcasted_iota(jnp.int32, (rows, rows), 0)
    column = lax.broadcasted_iota(jnp.int32, (rows, rows), 1)
    if spatial:
        return row // S == column // S
    return row % S == column % S


VMEM_LIMIT = pltpu.CompilerParams(vmem_limit_bytes=48 * 1024 * 1024)


def self_attend(qkv, spatial):
    rows = F * S

    def kernel(qkv_ref, out_ref):
        attend_heads(qkv_ref, qkv_ref, D, qkv_ref, 2 * D, out_ref, same_group(rows, spatial))

    return pl.pallas_call(
        kernel,
        grid=(qkv.shape[0] // rows,),
        in_specs=[pl.BlockSpec((rows, 3 * D), lambda i: (i, 0))],
        out_specs=pl.BlockSpec((rows, D), lambda i: (i, 0)),
        out_shape=jax.ShapeDtypeStruct((qkv.shape[0], D), jnp.bfloat16),
        compiler_params=VMEM_LIMIT,
        name="self_attend",
    )(qkv)


def self_attend_back(qkv, grad_mix, spatial):
    rows = F * S

    def kernel(qkv_ref, grad_ref, out_ref):
        attend_heads_back(
            qkv_ref, qkv_ref, D, qkv_ref, 2 * D, grad_ref,
            out_ref, out_ref, out_ref, same_group(rows, spatial),
        )

    return pl.pallas_call(
        kernel,
        grid=(qkv.shape[0] // rows,),
        in_specs=[
            pl.BlockSpec((rows, 3 * D), lambda i: (i, 0)),
            pl.BlockSpec((rows, D), lambda i: (i, 0)),
        ],
        out_specs=pl.BlockSpec((rows, 3 * D), lambda i: (i, 0)),
        out_shape=jax.ShapeDtypeStruct(qkv.shape, jnp.bfloat16),
        compiler_params=VMEM_LIMIT,
        name="self_attend_back",
    )(qkv, grad_mix)


def caption_mask(length):
    return lax.broadcasted_iota(jnp.int32, (F * S, LCAP), 1) < length


def cross_attend(query, pairs, lengths):
    clips = pairs.shape[0]

    def kernel(length_ref, query_ref, pair_ref, out_ref):
        allowed = caption_mask(length_ref[pl.program_id(0)])
        attend_heads(query_ref, pair_ref.at[0], 0, pair_ref.at[0], D, out_ref, allowed)

    return pl.pallas_call(
        kernel,
        grid_spec=pltpu.PrefetchScalarGridSpec(
            num_scalar_prefetch=1,
            grid=(clips,),
            in_specs=[
                pl.BlockSpec((F * S, D), lambda i, lens: (i, 0)),
                pl.BlockSpec((1, LCAP, 2 * D), lambda i, lens: (i, 0, 0)),
            ],
            out_specs=pl.BlockSpec((F * S, D), lambda i, lens: (i, 0)),
        ),
        out_shape=jax.ShapeDtypeStruct(query.shape, jnp.bfloat16),
        compiler_params=VMEM_LIMIT,
        name="cross_attend",
    )(lengths, query, pairs)


def cross_attend_back(query, pairs, grad_mix, lengths):
    clips = pairs.shape[0]

    def kernel(length_ref, query_ref, pair_ref, grad_ref, grad_query_ref, grad_pair_ref):
        allowed = caption_mask(length_ref[pl.program_id(0)])
        attend_heads_back(
            query_ref, pair_ref.at[0], 0, pair_ref.at[0], D, grad_ref,
            grad_query_ref, grad_pair_ref.at[0], grad_pair_ref.at[0], allowed,
        )

    return pl.pallas_call(
        kernel,
        grid_spec=pltpu.PrefetchScalarGridSpec(
            num_scalar_prefetch=1,
            grid=(clips,),
            in_specs=[
                pl.BlockSpec((F * S, D), lambda i, lens: (i, 0)),
                pl.BlockSpec((1, LCAP, 2 * D), lambda i, lens: (i, 0, 0)),
                pl.BlockSpec((F * S, D), lambda i, lens: (i, 0)),
            ],
            out_specs=[
                pl.BlockSpec((F * S, D), lambda i, lens: (i, 0)),
                pl.BlockSpec((1, LCAP, 2 * D), lambda i, lens: (i, 0, 0)),
            ],
        ),
        out_shape=[
            jax.ShapeDtypeStruct(query.shape, jnp.bfloat16),
            jax.ShapeDtypeStruct(pairs.shape, jnp.bfloat16),
        ],
        compiler_params=VMEM_LIMIT,
        name="cross_attend_back",
    )(lengths, query, pairs, grad_mix)


class Place:
    def __init__(self):
        self.wide = lax.axis_size("wide")
        self.narrow = lax.axis_size("narrow")
        self.depth = self.wide // 4
        self.half = self.depth // 2
        self.at = lax.axis_index("wide")
        self.core = self.at & 1
        self.x = (self.at >> 1) & 1
        self.z = self.at >> 2
        self.y = lax.axis_index("narrow")

    def over_wide(self, values, bit):
        return lax.ppermute(values, "wide", [(i, i ^ bit) for i in range(self.wide)])

    def over_core(self, values):
        return self.over_wide(values, 1)

    def over_x(self, values):
        return self.over_wide(values, 2)

    def over_z(self, values, bit):
        return self.over_wide(values, 4 * bit)

    def to_owner(self, values):
        pairs = [
            (i, i ^ 4 * self.half)
            for i in range(self.wide)
            if (i >> 2) // self.half != i & 1
        ]
        return lax.ppermute(values, "wide", pairs)

    def from_owner(self, values):
        pairs = [(i, i ^ 1) for i in range(self.wide) if (i >> 2) // self.half == i & 1]
        return lax.ppermute(values, "wide", pairs)

    def over_y(self, values, bit):
        return lax.ppermute(values, "narrow", [(i, i ^ bit) for i in range(self.narrow)])


def pair_up(bit, own, other):
    first = bit == 0
    return jnp.where(first, own, other), jnp.where(first, other, own)


def bits_of(size):
    return [1 << at for at in range(size.bit_length() - 1)]


def hold(values, others):
    if not others:
        return values
    kept, _ = lax.optimization_barrier((values, others))
    return kept


class Ticks:
    def __init__(self, joint):
        self.joint = joint
        self.ended = {True: [], False: []}
        self.sent = []

    def run(self, jobs, others=()):
        self.before = self.ended[True]
        ended = {True: [], False: []}
        before = dict(self.ended)
        if self.joint:
            before = {kind: list(before.values()) for kind in before}
            self.ended = {True: [], False: []}
        self.sent = []
        results = []
        for kind in (True, False):
            mine = [job for job in jobs if job.planar == kind]
            if not mine:
                continue
            values = [[value for value, _ in job.sends] for job in mine]
            values = hold(values, [before[kind], list(others)])
            self.sent.append(values)
            for job, held in zip(mine, values):
                result = [exchange(value) for value, (_, exchange) in zip(held, job.sends)]
                ended[kind].append(result)
                results.append((job, result))
            self.ended[kind] = ended[kind]
        for job, result in results:
            job.take(result)

    def during(self, values):
        return hold(values, [self.sent, self.before])

    def after(self, values):
        return hold(values, self.ended[True])


class Job:
    planar = False

    def __init__(self, transfers):
        self.transfers = transfers
        self.sends = next(transfers)

    def take(self, results):
        try:
            self.sends = self.transfers.send(results)
        except StopIteration:
            self.sends = None


def spread_y(place, values):
    pieces = [values]
    for bit in bits_of(place.narrow):
        pieces = pieces + [place.over_y(piece, bit) for piece in pieces]
    return pieces[1:]


class Gather(Job):
    def __init__(self, place, own):
        self.place = place
        super().__init__(self.plan(own[None]))

    def plan(self, block):
        place = self.place
        half = place.half
        rows, width = block.shape[1:]
        self.folded = place.narrow == 2 and width % 128 != 0 and rows % 16 == 0
        if self.folded:
            block = jnp.concatenate([block[:, : rows // 2], block[:, rows // 2 :]], axis=-1)
        for bit in bits_of(half):
            [other] = yield [(block, lambda values, bit=bit: place.over_z(values, bit))]
            block = jnp.concatenate(pair_up(place.z & bit, block, other))
        quarter = half // 2
        low, high = block[:quarter], block[quarter:]
        [low_away] = yield [(low, lambda values: place.over_z(values, half))]
        [high_away] = yield [(high, lambda values: place.over_z(values, half))]
        low = pair_up(place.z & half, low, low_away)
        high = pair_up(place.z & half, high, high_away)
        block = jnp.concatenate([low[0], high[0], low[1], high[1]])
        self.planar = True
        by_x, by_y = yield [(block, place.over_x), (block, lambda values: spread_y(place, values))]
        far_xy, near_xy = yield [
            (jnp.stack([piece[half:] for piece in by_y]), place.over_x),
            (by_x[:half], lambda values: spread_y(place, values)),
        ]
        columns = width * place.narrow
        mine = unwritten((place.depth, 2, rows, columns))
        parts = (
            (0, 0, self.lanes([block] + list(by_y))),
            (0, 1, self.lanes([by_x[:half]] + list(near_xy))),
            (half, 1, self.lanes([by_x[half:]] + [far_xy[at] for at in range(place.narrow - 1)])),
        )
        for first_z, apart, part in parts:
            mine = lax.dynamic_update_slice(
                mine, part[:, None], (first_z, place.x ^ apart, 0, 0)
            )
        self.mine = mine
        self.planar = False
        [self.other] = yield [(mine, place.over_core)]

    def lanes(self, pieces):
        place = self.place
        if place.narrow == 1:
            return pieces[0]
        if self.folded:
            low, high = pair_up(place.y, pieces[0], pieces[1])
            width = low.shape[-1] // 2
            return jnp.concatenate(
                [
                    jnp.concatenate([low[..., :width], high[..., :width]], axis=-1),
                    jnp.concatenate([low[..., width:], high[..., width:]], axis=-1),
                ],
                axis=-2,
            )
        if place.narrow == 2:
            return jnp.concatenate(pair_up(place.y, pieces[0], pieces[1]), axis=-1)
        return jnp.concatenate(
            [lax.select_n(place.y ^ spot, *pieces) for spot in range(place.narrow)], axis=-1
        )

    def whole(self, first_row, rows):
        place = self.place
        span = slice(first_row, first_row + rows)
        columns = self.mine.shape[-1]
        whole = unwritten((place.depth, 2, 2, rows, columns))
        for part, core in ((self.mine, place.core), (self.other, 1 - place.core)):
            whole = lax.dynamic_update_slice(
                whole, part[:, :, None, span], (0, 0, core, 0, 0)
            )
        return whole.reshape(place.wide * rows, columns)


def unwritten(shape):
    return pl.pallas_call(
        lambda out_ref: None,
        out_specs=pl.BlockSpec(memory_space=pl.ANY),
        out_shape=jax.ShapeDtypeStruct(shape, jnp.bfloat16),
        name="unwritten",
    )()


def side(values, bit, axis):
    return lax.dynamic_index_in_dim(values, bit, axis, keepdims=False)


def columns_at(values, index, count):
    width = values.shape[-1] // count
    if count == 1:
        return values
    if count == 2:
        return jnp.where(index == 0, values[..., :width], values[..., width:])
    return lax.dynamic_slice_in_dim(values, index * width, width, axis=values.ndim - 1)


def wide_float(values):
    return values.astype(jnp.float32)


def reduce_y(place, values):
    for bit in reversed(bits_of(place.narrow)):
        upper = ((place.y & bit) != 0).astype(jnp.int32)
        away = place.over_y(rounded(columns_at(values, 1 - upper, 2)), bit)
        values = columns_at(values, upper, 2) + wide_float(away)
    return values


class Scatter(Job):
    def __init__(self, place, products):
        self.place = place
        super().__init__(self.plan(products))

    def plan(self, products):
        place = self.place
        spread = place.half
        quarter = spread // 2
        sends = [(grad, place.over_core) for _, _, grad, *known in products if len(known) == 1]
        away = iter((yield sends) if sends else ())
        views = []
        for operand, operand_away, grad, parts, *known in products:
            grad_away = known[0] if known else next(away)
            kept = matmul_tn(columns_at(operand, place.core, 2), grad)
            total = matmul_tn(columns_at(operand_away, place.core, 2), grad_away)
            total = rounded(total + wide_float(rounded(kept)))
            width = grad.shape[1] // parts
            for part in range(parts):
                view = total[:, part * width : (part + 1) * width]
                views.append(view.reshape(spread, 2, -1, width))

        def summed(span, x_bit=None):
            mine = [view[span] for view in views]
            if x_bit is not None:
                mine = [side(view, x_bit, 1) for view in mine]
            return jnp.concatenate(mine, axis=-2) if len(mine) > 1 else mine[0]

        near_span, far_span = slice(0, quarter), slice(quarter, None)
        self.planar = True
        if place.narrow == 2:
            near_away, far_away = yield [
                (summed(near_span, 1 - place.x), place.over_x),
                (
                    columns_at(summed(far_span), 1 - place.y, 2),
                    lambda values: place.over_y(values, 1),
                ),
            ]

            def near(y_bit):
                mine = columns_at(summed(near_span, place.x), y_bit, 2)
                return wide_float(mine) + wide_float(columns_at(near_away, y_bit, 2))

            def far(x_bit):
                mine = columns_at(summed(far_span, x_bit), place.y, 2)
                return wide_float(mine) + wide_float(side(far_away, x_bit, 1))

            near_back, far_back = yield [
                (rounded(near(1 - place.y)), lambda values: place.over_y(values, 1)),
                (rounded(far(1 - place.x)), place.over_x),
            ]
            near = near(place.y) + wide_float(near_back)
            far = far(place.x) + wide_float(far_back)
        else:
            near_away, far = yield [
                (summed(near_span, 1 - place.x), place.over_x),
                (wide_float(summed(far_span)), lambda values: reduce_y(place, values)),
            ]
            near = wide_float(summed(near_span, place.x)) + wide_float(near_away)
            near, far_back = yield [
                (near, lambda values: reduce_y(place, values)),
                (rounded(side(far, 1 - place.x, 1)), place.over_x),
            ]
            far = side(far, place.x, 1) + wide_float(far_back)
        self.planar = False
        total, sent = pair_up(place.z & quarter, near, far)
        [away] = yield [(rounded(sent), lambda values: place.over_z(values, quarter))]
        total = total + wide_float(away)
        for bit in reversed(bits_of(quarter)):
            total = total.reshape((2, total.shape[0] // 2) + total.shape[1:])
            upper = ((place.z & bit) != 0).astype(jnp.int32)
            [away] = yield [
                (
                    rounded(side(total, 1 - upper, 0)),
                    lambda values, bit=bit: place.over_z(values, bit),
                )
            ]
            total = side(total, upper, 0) + wide_float(away)
        total = total[0]
        [away] = yield [(rounded(total), place.to_owner)]
        total = total + wide_float(away)
        pieces, first = [], 0
        for view in views:
            rows = view.shape[2]
            pieces.append(total[first : first + rows].reshape(2, rows // 2, -1))
            first += rows
        sent = [side(piece, 1 - place.core, 0) for piece in pieces]
        sent = jnp.concatenate(sent) if len(sent) > 1 else sent[0]
        [away] = yield [(sent, place.from_owner)]
        owner = place.z // spread == place.core
        self.total, first = [], 0
        for piece in pieces:
            rows = piece.shape[1]
            theirs = away[first : first + rows]
            self.total.append(jnp.where(owner, side(piece, place.core, 0), theirs))
            first += rows


class Reducer:
    def __init__(self, place):
        self.place = place
        self.ticks = Ticks(False)
        self.jobs = []

    def add(self, *products):
        job = Scatter(self.place, products)
        self.jobs.append(job)
        return job

    def run(self, *others, wait=()):
        due = [job for job in self.jobs if job.sends is not None and job not in wait]
        if due:
            self.ticks.run(due, others)
        return bool(due)


def adam_update(master, first_moment, second_moment, gradient, step_value):
    first_new = 0.9 * first_moment + 0.1 * gradient
    second_new = 0.999 * second_moment + 0.001 * gradient * gradient
    first_hat = first_new / (1.0 - 0.9**step_value)
    second_hat = second_new / (1.0 - 0.999**step_value)
    master_new = master - LEARNING_RATE * (
        first_hat / (jnp.sqrt(second_hat) + 1e-08) + 0.01 * master
    )
    return (master_new, first_new, second_new)


def body(
    projections,
    qkv_weights,
    mlp_weights,
    ada_weights,
    entry_weights,
    patch_weights,
    shift_tables,
    first_projections,
    first_qkv_weights,
    first_mlp_weights,
    first_ada_weights,
    first_entry_weights,
    first_patch_weights,
    first_shift_tables,
    second_projections,
    second_qkv_weights,
    second_mlp_weights,
    second_ada_weights,
    second_entry_weights,
    second_patch_weights,
    second_shift_tables,
    latents,
    noise,
    captions,
    cap_len,
    timesteps,
    step_count,
):
    shards = (
        projections,
        qkv_weights,
        mlp_weights,
        ada_weights,
        entry_weights,
        patch_weights,
        shift_tables,
    )
    firsts = (
        first_projections,
        first_qkv_weights,
        first_mlp_weights,
        first_ada_weights,
        first_entry_weights,
        first_patch_weights,
        first_shift_tables,
    )
    seconds = (
        second_projections,
        second_qkv_weights,
        second_mlp_weights,
        second_ada_weights,
        second_entry_weights,
        second_patch_weights,
        second_shift_tables,
    )
    place = Place()
    clips = latents.shape[0]
    tokens = F * S
    video_count = clips * place.wide * place.narrow
    rows = projections.shape[1]
    entry_rows = entry_weights.shape[0]

    def by_clip(values):
        return values.reshape(clips, tokens, values.shape[-1])

    def flat(values):
        return values.reshape(clips * tokens, values.shape[-1])

    devices = place.wide * place.narrow
    all_clips = clips * devices

    def to_all(values):
        return lax.all_to_all(values, ("wide", "narrow"), split_axis=0, concat_axis=0, tiled=True)

    def columns_to_all(values):
        pieces = values.reshape(values.shape[0], place.narrow, -1).transpose(1, 0, 2)
        pieces = jnp.broadcast_to(pieces[None], (place.wide,) + pieces.shape)
        return to_all(pieces.reshape((devices,) + pieces.shape[2:]))

    proj_low, qkv_low, mlp_low, ada_low, entry_low, patch_low, table_low = (
        rounded(shard) for shard in shards
    )
    width = projections.shape[2]
    small = jnp.concatenate([patch_low.reshape(-1), table_low.reshape(-1)])
    small_rows = -(-small.shape[0] // (8 * width)) * 8
    small = jnp.pad(small, (0, small_rows * width - small.shape[0])).reshape(small_rows, width)
    ticks = Ticks(True)
    gathers = [
        Gather(place, own)
        for own in (
            jnp.concatenate([proj_low[:2].reshape(2 * rows, width), small]),
            entry_low,
            qkv_low.reshape(2 * rows, -1),
            proj_low[2:].reshape(6 * rows, width),
            mlp_low[0],
            mlp_low[1],
        )
    ]
    early, entry_gather, qkv_gather, late, mlp_in_gather, mlp_out_gather = gathers
    rounds = iter(range(2 * len(gathers) + len(bits_of(place.depth)) + 4))

    def gather_on(*others):
        now = next(rounds)
        due = [job for at, job in enumerate(gathers) if job.sends is not None and now >= 2 * at]
        if due:
            ticks.run(due, others)

    while early.sends is not None:
        gather_on()
    small_all = early.whole(2 * rows, small_rows)
    proj_all = [early.whole(0, rows), early.whole(rows, rows)]
    small_all = small_all.reshape(place.wide, small_rows, place.narrow, width).transpose(0, 2, 1, 3)
    small_all = small_all.reshape(place.wide, place.narrow, small_rows * width)
    patch_count = patch_low.size
    patch_all = small_all[:, :, :patch_count].reshape(
        (place.wide, place.narrow) + patch_low.shape
    )
    patch_all = patch_all.transpose(2, 0, 3, 1, 4).reshape(2, D, -1)
    table_all = small_all[:, :, patch_count : patch_count + table_low.size].reshape(
        (place.wide, place.narrow) + table_low.shape
    )
    table_all = table_all.transpose(1, 2, 0, 3).reshape(8, D).astype(jnp.float32)

    time_value = timesteps.astype(jnp.float32)
    signal = jnp.cos((time_value / 1000.0 + 0.008) / 1.008 * (math.pi / 2)) ** 2
    noise_rows = flat(noise.astype(jnp.float32))
    noised_low = rounded(
        flat(
            jnp.sqrt(signal)[:, None, None] * latents.astype(jnp.float32)
            + jnp.sqrt(1.0 - signal)[:, None, None] * noise.astype(jnp.float32)
        )
    )
    spatial_pos = jnp.tile(sinusoid(jnp.arange(S, dtype=jnp.float32), D), (clips * F, 1))
    frame_pos = jnp.tile(jnp.repeat(sinusoid(jnp.arange(F, dtype=jnp.float32), D), S, 0), (clips, 1))
    embed_low = rounded(sinusoid(time_value, FREQ))
    while entry_gather.sends is not None:
        gather_on(patch_all, table_all)
    gather_on()
    entry_gather.other = ticks.during(entry_gather.other)
    entry_all = entry_gather.whole(0, entry_rows)
    time_inner = matmul(embed_low, entry_all[CAP:])
    inner_low = rounded(jax.nn.silu(time_inner))
    time_embed = matmul(inner_low, proj_all[0])
    embed_act = rounded(jax.nn.silu(time_embed))

    def by_rows(values):
        return values.reshape(clips, place.wide, rows).transpose(1, 0, 2)

    sent = jnp.concatenate(
        [
            by_rows(embed_act),
            by_rows(inner_low),
            jnp.broadcast_to(embed_low[None], (place.wide,) + embed_low.shape),
        ],
        axis=-1,
    )
    sent = jnp.broadcast_to(sent[:, None], (place.wide, place.narrow) + sent.shape[1:])
    gather_on(sent, entry_all)
    sent = ticks.during(sent)
    sent = to_all(sent.reshape((devices,) + sent.shape[2:])).reshape(all_clips, -1)
    my_embed_act, my_inner, embed_all = sent[:, :rows], sent[:, rows : 2 * rows], sent[:, 2 * rows :]
    part = matmul(my_embed_act, ada_low).reshape(devices, clips, -1)

    caption_rows = captions.reshape(clips * LCAP, CAP)
    caption_wide = jnp.pad(caption_rows, ((0, 0), (0, place.wide * entry_rows - CAP)))
    caption_inner = matmul(ticks.during(caption_rows), entry_all[:CAP])
    caption_act = rounded(jax.nn.gelu(caption_inner))
    context_low = rounded(matmul(caption_act, proj_all[1]))
    gather_on(context_low)
    part = to_all(ticks.during(part))
    qkv_gather.other = ticks.during(qkv_gather.other)
    qkv_all = [qkv_gather.whole(0, rows), qkv_gather.whole(rows, rows)]
    part = part.reshape(place.wide, place.narrow, clips, -1)
    modulations = jnp.sum(part, axis=0).transpose(1, 0, 2).reshape(clips, 6, D) + table_all[:6]
    caption_wide_away = place.over_core(caption_wide)
    caption_act_away = place.over_core(caption_act)
    context_low_away = place.over_core(context_low)
    gather_on(modulations, caption_wide_away, caption_act_away, context_low_away, *qkv_all)
    modulations = ticks.during(modulations)
    shift_a, scale_a, gate_a, shift_m, scale_m, gate_m = (
        modulations[:, at : at + 1] for at in range(6)
    )
    final_shift = (time_embed + table_all[6])[:, None]
    final_scale = (time_embed + table_all[7])[:, None]

    hidden = matmul_nt(noised_low, patch_all[0]) + spatial_pos
    normed_spatial = rounded(flat(modulate(by_clip(hidden), shift_a, scale_a)))
    spatial_qkv = rounded(matmul(normed_spatial, qkv_all[0]))
    normed_spatial_away = place.over_core(normed_spatial)
    gather_on(spatial_qkv, normed_spatial_away)
    late.other = ticks.during(late.other)
    proj_all = proj_all + [late.whole(at * rows, rows) for at in range(6)]
    pair_weight = jnp.concatenate([proj_all[5], proj_all[6]], axis=1)
    spatial_mix = self_attend(ticks.during(spatial_qkv), True)
    gather_on(spatial_mix, pair_weight, *proj_all)
    spatial_mix, context_low = ticks.during((spatial_mix, context_low))
    cross_pairs = rounded(matmul(context_low, pair_weight))
    spatial_out = matmul(spatial_mix, proj_all[2])
    hidden_one = hidden + flat(gate_a * by_clip(spatial_out))
    temporal_in = rounded(hidden_one + frame_pos)
    temporal_qkv = rounded(matmul(temporal_in, qkv_all[1]))
    spatial_mix_away = place.over_core(spatial_mix)
    temporal_in_away = place.over_core(temporal_in)
    gather_on(cross_pairs, temporal_qkv, spatial_mix_away, temporal_in_away)
    temporal_mix = self_attend(ticks.during(temporal_qkv), False)
    mlp_in_gather.other = ticks.during(mlp_in_gather.other)
    mlp_in = mlp_in_gather.whole(0, rows)
    temporal_out = matmul(temporal_mix, proj_all[3])
    hidden_two = hidden_one + flat(gate_a * by_clip(temporal_out))
    hidden_two_low = rounded(hidden_two)
    temporal_mix_away = place.over_core(temporal_mix)
    hidden_two_low_away = place.over_core(hidden_two_low)
    cross_query = rounded(matmul(hidden_two_low, proj_all[4]))
    while mlp_out_gather.sends is not None:
        gather_on(cross_query, mlp_in)
    mlp_out = mlp_out_gather.whole(0, rows)
    cross_mix = cross_attend(cross_query, cross_pairs.reshape(clips, LCAP, 2 * D), cap_len)
    cross_mix_away = place.over_core(cross_mix)
    hidden_three = hidden_two + matmul(cross_mix, proj_all[7])
    normed_mlp = rounded(flat(modulate(by_clip(hidden_three), shift_m, scale_m)))
    normed_mlp_away = place.over_core(normed_mlp)
    expand = matmul(normed_mlp, mlp_in)
    expand_act = rounded(jax.nn.gelu(expand))
    expand_act_away = place.over_core(expand_act)
    contract = matmul_nt(expand_act, mlp_out)
    hidden_four = hidden_three + flat(gate_m * by_clip(contract))
    final_low = rounded(flat(modulate(by_clip(hidden_four), final_shift, final_scale)))
    misfit = matmul(final_low, patch_all[1]) - noise_rows
    entries = tokens * latents.shape[2]
    loss_value = jnp.sum(misfit * misfit) / (entries * video_count)

    grad_pred = rounded(2.0 * misfit / (entries * video_count))
    grad_patch_out = matmul_tn(final_low, grad_pred)
    _, pull_final = jax.vjp(modulate, by_clip(hidden_four), final_shift, final_scale)
    grad_four, grad_fshift, grad_fscale = pull_final(by_clip(matmul_nt(grad_pred, patch_all[1])))
    grad_contract = rounded(flat(grad_four * gate_m))
    grad_gate_mlp = jnp.sum(grad_four * by_clip(contract), axis=1)
    reducer = Reducer(place)
    during, after = reducer.ticks.during, reducer.ticks.after
    grad_contract_away = place.over_core(grad_contract)
    mlp_out_scatter = reducer.add(
        (grad_contract, grad_contract_away, expand_act, 1, expand_act_away)
    )
    reducer.run()
    _, pull_gelu = jax.vjp(jax.nn.gelu, expand)
    grad_expand = rounded(pull_gelu(matmul(during(grad_contract), mlp_out))[0])
    mlp_in_scatter = reducer.add((normed_mlp, normed_mlp_away, grad_expand, 1))
    reducer.run()
    _, pull_mlp_norm = jax.vjp(modulate, by_clip(hidden_three), shift_m, scale_m)
    grad_three_part, grad_shift_mlp, grad_scale_mlp = pull_mlp_norm(
        by_clip(matmul_nt(during(grad_expand), mlp_in))
    )
    grad_three = flat(grad_four + grad_three_part)
    grad_cross_out = rounded(grad_three)
    reducer.run(grad_cross_out)
    grad_cross_mix = rounded(matmul_nt(during(grad_cross_out), proj_all[7]))
    grad_query_low, grad_pairs_low = cross_attend_back(
        cross_query, cross_pairs.reshape(clips, LCAP, 2 * D), grad_cross_mix, cap_len
    )
    grad_pairs_low = grad_pairs_low.reshape(clips * LCAP, 2 * D)
    grad_context = rounded(matmul_nt(grad_pairs_low, pair_weight))
    caption_scatter = reducer.add(
        (caption_act, caption_act_away, grad_context, 1),
        (context_low, context_low_away, grad_pairs_low, 2),
    )
    reducer.run(grad_query_low)
    _, pull_caption = jax.vjp(jax.nn.gelu, caption_inner)
    grad_context, grad_query_low = during((grad_context, grad_query_low))
    grad_caption_inner = rounded(pull_caption(matmul_nt(grad_context, proj_all[1]))[0])
    grad_two = grad_three + matmul_nt(grad_query_low, proj_all[4])
    grad_temporal_out = rounded(flat(by_clip(grad_two) * gate_a))
    grad_gate_attn = jnp.sum(by_clip(grad_two * temporal_out), axis=1)
    grad_temporal_mix = rounded(matmul_nt(grad_temporal_out, proj_all[3]))
    reducer.run(grad_temporal_mix, grad_caption_inner)
    grad_temporal_qkv = self_attend_back(temporal_qkv, during(grad_temporal_mix), False)
    entry_scatter = reducer.add((caption_wide, caption_wide_away, grad_caption_inner, 1))
    qkv_one_scatter = reducer.add((temporal_in, temporal_in_away, grad_temporal_qkv, 1))
    reducer.run()
    grad_one = grad_two + matmul_nt(during(grad_temporal_qkv), qkv_all[1])
    grad_spatial_out = rounded(flat(by_clip(grad_one) * gate_a))
    grad_gate_attn = grad_gate_attn + jnp.sum(by_clip(grad_one * spatial_out), axis=1)
    grad_spatial_mix = rounded(matmul_nt(grad_spatial_out, proj_all[2]))
    reducer.run(grad_spatial_mix, wait=(qkv_one_scatter,))
    grad_spatial_qkv = self_attend_back(spatial_qkv, during(grad_spatial_mix), True)
    qkv_zero_scatter = reducer.add((normed_spatial, normed_spatial_away, grad_spatial_qkv, 1))
    reducer.run(wait=(qkv_one_scatter,))
    grad_normed_spatial = matmul_nt(during(grad_spatial_qkv), qkv_all[0])
    square_scatter = reducer.add(
        (spatial_mix, spatial_mix_away, grad_spatial_out, 1),
        (temporal_mix, temporal_mix_away, grad_temporal_out, 1),
        (hidden_two_low, hidden_two_low_away, grad_query_low, 1),
        (cross_mix, cross_mix_away, grad_cross_out, 1),
    )
    reducer.run(grad_normed_spatial, wait=(qkv_zero_scatter,))
    grad_normed_spatial = during(grad_normed_spatial)
    reducer.run(wait=(qkv_zero_scatter, square_scatter))
    reducer.run(wait=(square_scatter,))
    qkv_zero_started = reducer.ticks.sent
    reducer.run(wait=(square_scatter,))
    reducer.run()
    middle = reducer.ticks.sent
    while reducer.run():
        pass
    sum_mlp_in, sum_mlp_out = mlp_in_scatter.total[0], mlp_out_scatter.total[0]
    sum_qkv_one = qkv_one_scatter.total[0]
    sum_qkv_zero = qkv_zero_scatter.total[0]
    sum_two, sum_three, sum_four, sum_seven = square_scatter.total
    sum_one, sum_five, sum_six = caption_scatter.total
    sum_entry = entry_scatter.total[0]
    _, pull_spatial_norm = jax.vjp(modulate, by_clip(hidden), shift_a, scale_a)
    grad_hidden_part, grad_shift_attn, grad_scale_attn = pull_spatial_norm(
        by_clip(grad_normed_spatial)
    )
    grad_hidden = rounded(grad_one + flat(grad_hidden_part))
    grad_patch_in = matmul_tn(grad_hidden, noised_low)
    grad_modulations = jnp.stack(
        [
            grad_shift_attn[:, 0],
            grad_scale_attn[:, 0],
            grad_gate_attn,
            grad_shift_mlp[:, 0],
            grad_scale_mlp[:, 0],
            grad_gate_mlp,
        ],
        axis=1,
    )

    grad_ada_out = hold(rounded(grad_modulations.reshape(clips, 6 * D)), qkv_zero_started)
    grad_ada_mine = columns_to_all(grad_ada_out).reshape(all_clips, -1)
    grad_ada = matmul_tn(my_embed_act, grad_ada_mine)
    grad_ada_mine = hold(grad_ada_mine, middle)
    act_part = to_all(matmul_nt(grad_ada_mine, ada_low).reshape(devices, clips, rows))
    act_part = jnp.sum(act_part.reshape(place.wide, place.narrow, clips, rows), axis=1)
    grad_embed_act = act_part.transpose(1, 0, 2).reshape(clips, D)
    _, pull_embed = jax.vjp(jax.nn.silu, time_embed)
    grad_time_embed = rounded(
        pull_embed(grad_embed_act)[0] + (grad_fshift + grad_fscale)[:, 0]
    )
    _, pull_inner = jax.vjp(jax.nn.silu, time_inner)
    grad_time_inner = rounded(pull_inner(matmul_nt(grad_time_embed, proj_all[0]))[0])
    time_rows = columns_to_all(jnp.concatenate([grad_time_embed, grad_time_inner]))
    grad_embed_mine = time_rows[:, :clips].reshape(all_clips, width)
    grad_inner_mine = time_rows[:, clips:].reshape(all_clips, width)
    grad_proj_zero = matmul_tn(my_inner, grad_embed_mine)
    grad_time_rows = matmul_tn(embed_all, grad_inner_mine)
    spot = jnp.clip((place.at + 1) * entry_rows - CAP, 0, FREQ + entry_rows)
    padded_rows = jnp.pad(grad_time_rows, ((entry_rows, entry_rows), (0, 0)))
    grad_entry_time = lax.dynamic_slice_in_dim(padded_rows, spot, entry_rows, axis=0)

    grad_tables = jnp.concatenate(
        [
            jnp.sum(grad_modulations, axis=0),
            jnp.sum(grad_fshift, axis=0),
            jnp.sum(grad_fscale, axis=0),
        ]
    )
    grad_patches = jnp.stack([grad_patch_in, grad_patch_out]).reshape(
        2, place.wide, rows, place.narrow, -1
    )
    grad_tables = grad_tables.reshape(place.narrow, -1, place.wide, rows)
    small_grads = jnp.concatenate(
        [
            grad_patches.transpose(1, 3, 0, 2, 4).reshape(devices, -1),
            grad_tables.transpose(2, 0, 1, 3).reshape(devices, -1),
        ],
        axis=1,
    )
    small_grads = jnp.sum(to_all(hold(small_grads, middle)), axis=0)
    sum_patch = small_grads[: patch_weights.size].reshape(patch_weights.shape)
    sum_tables = small_grads[patch_weights.size :].reshape(shift_tables.shape)

    sum_projections = jnp.stack(
        [
            grad_proj_zero,
            sum_one,
            sum_two,
            sum_three,
            sum_four,
            sum_five,
            sum_six,
            sum_seven,
        ]
    )
    summed = (
        sum_projections,
        jnp.stack([sum_qkv_zero, sum_qkv_one]),
        jnp.stack([sum_mlp_in, sum_mlp_out]),
        grad_ada,
        sum_entry + grad_entry_time,
        sum_patch,
        sum_tables,
    )
    square_part = sum((jnp.sum(piece * piece) for piece in summed))
    both = jnp.broadcast_to(jnp.stack([loss_value, square_part]), (devices, 2))
    loss_total, square_total = jnp.sum(to_all(both), axis=0)
    grad_norm = jnp.sqrt(square_total)
    threshold = (video_count * latents.shape[1]) ** (-0.5)
    factor = threshold / jnp.maximum(grad_norm, threshold)
    step_value = step_count[0].astype(jnp.float32)
    updated = [
        adam_update(master, first_moment, second_moment, gradient * factor, step_value)
        for master, first_moment, second_moment, gradient in zip(shards, firsts, seconds, summed)
    ]
    return (
        updated[0][0],
        updated[1][0],
        updated[2][0],
        updated[3][0],
        updated[4][0],
        updated[5][0],
        updated[6][0],
        updated[0][1],
        updated[1][1],
        updated[2][1],
        updated[3][1],
        updated[4][1],
        updated[5][1],
        updated[6][1],
        updated[0][2],
        updated[1][2],
        updated[2][2],
        updated[3][2],
        updated[4][2],
        updated[5][2],
        updated[6][2],
        loss_total,
        grad_norm,
    )


def solution(mesh):
    return jax.shard_map(
        body,
        mesh=mesh,
        in_specs=(
            P(None, "wide", "narrow"),
            P(None, "wide", "narrow"),
            P(None, "wide", "narrow"),
            P("wide", "narrow"),
            P("wide", "narrow"),
            P(None, "wide", "narrow"),
            P("narrow", "wide"),
            P(None, "wide", "narrow"),
            P(None, "wide", "narrow"),
            P(None, "wide", "narrow"),
            P("wide", "narrow"),
            P("wide", "narrow"),
            P(None, "wide", "narrow"),
            P("narrow", "wide"),
            P(None, "wide", "narrow"),
            P(None, "wide", "narrow"),
            P(None, "wide", "narrow"),
            P("wide", "narrow"),
            P("wide", "narrow"),
            P(None, "wide", "narrow"),
            P("narrow", "wide"),
            P(("wide", "narrow"), None, None),
            P(("wide", "narrow"), None, None),
            P(("wide", "narrow"), None, None),
            P(("wide", "narrow")),
            P(("wide", "narrow")),
            P(),
        ),
        out_specs=(
            P(None, "wide", "narrow"),
            P(None, "wide", "narrow"),
            P(None, "wide", "narrow"),
            P("wide", "narrow"),
            P("wide", "narrow"),
            P(None, "wide", "narrow"),
            P("narrow", "wide"),
            P(None, "wide", "narrow"),
            P(None, "wide", "narrow"),
            P(None, "wide", "narrow"),
            P("wide", "narrow"),
            P("wide", "narrow"),
            P(None, "wide", "narrow"),
            P("narrow", "wide"),
            P(None, "wide", "narrow"),
            P(None, "wide", "narrow"),
            P(None, "wide", "narrow"),
            P("wide", "narrow"),
            P("wide", "narrow"),
            P(None, "wide", "narrow"),
            P("narrow", "wide"),
            P(),
            P(),
        ),
        check_vma=False,
    )
```
